32 devices in a mesh: dp: 16 (over z, y, x), tensor: 2 (over core).
Axes of the slice: x: 2, y: 2, z: 4, core: 2. Of those that a mesh axis runs over, the one named last changes fastest.
Arguments:
- tokens: bfloat16 [24576, 768], P('dp'), may hold values from -6 to 6
- lengths: int32 [48], P('dp'), may hold values from 64 to 512
- w_query: bfloat16 [768, 768], P(None, 'tensor'), may hold values from -0.3125 to 0.3125
- b_query: float32 [768], P('tensor'), may hold values from -1.75 to 1.75
- w_key: bfloat16 [768, 768], P(None, 'tensor'), may hold values from -0.3125 to 0.3125
- w_value: bfloat16 [768, 768], P(None, 'tensor'), may hold values from -0.21875 to 0.21875
- b_value: float32 [768], P('tensor'), may hold values from -1.75 to 1.75
- w_out: bfloat16 [768, 768], P('tensor'), may hold values from -0.875 to 0.875
- b_out: float32 [768], replicated, may hold values from -1.75 to 1.75
- gain_one: float32 [768], replicated, may hold values from 0.25 to 1.75
- bias_one: float32 [768], replicated, may hold values from -1.75 to 1.75
- w_up: bfloat16 [768, 3072], P(None, 'tensor'), may hold values from -0.21875 to 0.21875
- b_up: float32 [3072], P('tensor'), may hold values from -1.75 to 1.75
- w_down: bfloat16 [3072, 768], P('tensor'), may hold values from -0.109375 to 0.109375
- b_down: float32 [768], replicated, may hold values from -1.75 to 1.75
- gain_two: float32 [768], replicated, may hold values from 0.25 to 1.75
- bias_two: float32 [768], replicated, may hold values from -1.75 to 1.75
- w_proj: bfloat16 [768, 128], replicated, may hold values from -0.21875 to 0.21875
- b_proj: float32 [128], replicated, may hold values from -1.75 to 1.75
- cotangent: bfloat16 [24576, 128], P('dp'), may hold values from -6 to 6
Outputs:
- embeddings: bfloat16 [24576, 128], P('dp')
- grad_tokens: float32 [24576, 768], P('dp')
- grad_w_query: float32 [768, 768], P(None, 'tensor')
- grad_b_query: float32 [768], P('tensor')
- grad_w_key: float32 [768, 768], P(None, 'tensor')
- grad_w_value: float32 [768, 768], P(None, 'tensor')
- grad_b_value: float32 [768], P('tensor')
- grad_w_out: float32 [768, 768], P('tensor')
- grad_b_out: float32 [768], replicated
- grad_gain_one: float32 [768], replicated
- grad_bias_one: float32 [768], replicated
- grad_w_up: float32 [768, 3072], P(None, 'tensor')
- grad_b_up: float32 [3072], P('tensor')
- grad_w_down: float32 [3072, 768], P('tensor')
- grad_b_down: float32 [768], replicated
- grad_gain_two: float32 [768], replicated
- grad_bias_two: float32 [768], replicated
- grad_w_proj: float32 [768, 128], replicated
- grad_b_proj: float32 [128], replicated
The draws below stay inside these ranges and needn't reach their ends.
All inputs are finite; a program needn't handle non-finite values.
Results may differ from the reference program's by a relative error of at most 0.023.
Values may be sent and summed in bfloat16 or wider, within the bound.
No kernel may reach another device: no remote copies, remote signals or barrier semaphores. Data moves between devices by JAX's collectives and lax.ppermute only.
A program may use at most 256 MiB of HBM per device.

```python
import jax
import jax.numpy as jnp
from jax import lax

D = 768
HEADS = 12
HEAD = 64
FF = 3072
PROJ = 128
SEQ_LEN = 512
SEQS = 48
TOKENS = 24576
N_TENSOR = 2


def draw_lengths(key, part):
    lowest = SEQ_LEN // 8
    sampled = jax.random.randint(key, (SEQS,), lowest, SEQ_LEN + 1, dtype=jnp.int32)
    sampled = sampled.at[0].set(SEQ_LEN)
    return sampled.at[1].set(lowest)


def steps_of(key, dims, shards, least, top_value):
    gain, own = 1.0, jax.random.fold_in(key, 6)
    for position, blocks in shards:
        draws = jnp.exp(jax.random.uniform(jax.random.fold_in(own, position), (blocks,), jnp.float32, least / len(shards), top_value / len(shards)))
        gain = gain * jnp.repeat(draws, dims[position] // blocks).reshape([-1 if axis == position else 1 for axis in range(len(dims))])
    return gain


def centred(stream_key, shape, width, limit, shards=(), kind=jnp.bfloat16):
    gain = steps_of(stream_key, shape, shards, -0.22, 0.18) if shards else 1.0
    entries = jax.random.normal(stream_key, shape, jnp.float32) * width * gain
    return jnp.minimum(jnp.maximum(entries, -limit), limit).astype(kind)


def setup_inputs(seed: int = 0) -> dict:
    key_list = jax.random.split(jax.random.key(seed), 21)
    return {
        "tokens": centred(key_list[0], (TOKENS, D), 1.0, 6.0, ((0, 16),)),
        "lengths": draw_lengths(jax.random.fold_in(key_list[20], 71), 0),
        "w_query": centred(key_list[2], (D, D), (D // 2) ** -0.5, 0.3125, ((1, 2),)),
        "b_query": centred(key_list[3], (D,), 0.3, 1.75, ((0, 2),), jnp.float32),
        "w_key": centred(key_list[4], (D, D), (D // 2) ** -0.5, 0.3125, ((1, 2),)),
        "w_value": centred(key_list[5], (D, D), D ** -0.5, 0.21875, ((1, 2),)),
        "b_value": centred(key_list[6], (D,), 0.3, 1.75, ((0, 2),), jnp.float32),
        "w_out": centred(key_list[7], (D, D), (D // 16) ** -0.5, 0.875, ((0, 2),)),
        "b_out": centred(key_list[8], (D,), 0.3, 1.75, (), jnp.float32),
        "gain_one": jnp.clip(1.0 + 0.15 * jax.random.normal(key_list[9], (D,), jnp.float32), 0.25, 1.75),
        "bias_one": centred(key_list[10], (D,), 0.3, 1.75, (), jnp.float32),
        "w_up": centred(key_list[11], (D, FF), D ** -0.5, 0.21875, ((1, 2),)),
        "b_up": centred(key_list[12], (FF,), 0.3, 1.75, ((0, 2),), jnp.float32),
        "w_down": centred(key_list[13], (FF, D), FF ** -0.5, 0.109375, ((0, 2),)),
        "b_down": centred(key_list[14], (D,), 0.3, 1.75, (), jnp.float32),
        "gain_two": jnp.clip(1.0 + 0.15 * jax.random.normal(key_list[15], (D,), jnp.float32), 0.25, 1.75),
        "bias_two": centred(key_list[16], (D,), 0.3, 1.75, (), jnp.float32),
        "w_proj": centred(key_list[17], (D, PROJ), D ** -0.5, 0.21875),
        "b_proj": centred(key_list[18], (PROJ,), 0.3, 1.75, (), jnp.float32),
        "cotangent": centred(key_list[19], (TOKENS, PROJ), 1.0, 6.0, ((0, 16),)),
    }


EPS_NORM = 1e-12
EPS_UNIT = 1e-06
PRECISE = lax.Precision.HIGHEST

@jax.custom_vjp
def low(v):
    return lax.optimization_barrier(v.astype(jnp.bfloat16)).astype(jnp.float32)

@jax.custom_vjp
def low_back(v):
    return v

def low_keep(v):
    return (low(v), None)

def low_pass(kept, grad):
    return (grad,)

def back_keep(v):
    return (v, None)

def back_low(kept, grad):
    return (low(grad),)
low.defvjp(low_keep, low_pass)
low_back.defvjp(back_keep, back_low)

def matmul(operand, other):
    return jnp.dot(operand, other, precision=PRECISE, preferred_element_type=jnp.float32)

def layer_norm(residual, scale_gain, offset):
    center = residual - lax.optimization_barrier(jnp.mean(residual, axis=-1, keepdims=True))
    spread = lax.optimization_barrier(jnp.mean(center * center, axis=-1, keepdims=True))
    return center * lax.rsqrt(spread + EPS_NORM) * scale_gain + offset

def unit_rows(embedding):
    return embedding * lax.rsqrt(lax.optimization_barrier(jnp.sum(embedding * embedding, axis=-1, keepdims=True)) + EPS_UNIT)

def attend(pieces):
    queries, key_rows, values, limits = pieces
    scores = jnp.einsum('gqhd,gkhd->ghqk', queries, key_rows, precision=PRECISE) * 0.125
    places = jnp.arange(queries.shape[1], dtype=jnp.int32)
    visible = places[None, :] < limits[:, None]
    scores = jnp.where(visible[:, None, None, :], scores, -1000000000.0)
    scores = low_back(scores)
    weights = low(jax.nn.softmax(scores, axis=-1))
    context = jnp.einsum('ghqk,gkhd->gqhd', weights, values, precision=PRECISE)
    return low_back(low(context))

def grouped(operand, other):
    group_width = operand.shape[1] // N_TENSOR
    summed = jnp.zeros((operand.shape[0], other.shape[1]), jnp.float32)
    for group_idx in range(N_TENSOR):
        first = group_idx * group_width
        summed = summed + low(matmul(operand[:, first:first + group_width], other[first:first + group_width]))
    return summed

def reference(tokens, lengths, w_query, b_query, w_key, w_value, b_value, w_out, b_out, gain_one, bias_one, w_up, b_up, w_down, b_down, gain_two, bias_two, w_proj, b_proj, cotangent):
    per_block = 8
    blocks = SEQS // per_block
    seq_shape = (blocks, per_block, SEQ_LEN, HEADS, HEAD)

    def forward(parameters):
        inputs, query_w, query_b, key_w, value_w, value_b, out_w, out_b, gain_a, bias_a, up_w, up_b, down_w, down_b, gain_b, bias_b, proj_w, proj_b = parameters
        queries = low(low_back(matmul(inputs, query_w)) + query_b)
        key_rows = low(low_back(matmul(inputs, key_w)))
        values = low(low_back(matmul(inputs, value_w)) + value_b)
        context = lax.map(jax.checkpoint(attend), (queries.reshape(seq_shape), key_rows.reshape(seq_shape), values.reshape(seq_shape), lengths.reshape(blocks, per_block)))
        context = context.reshape(TOKENS, D)
        attn_out = low_back(grouped(context, out_w)) + out_b
        hidden_a = layer_norm(inputs + attn_out, gain_a, bias_a)
        pre_act = low_back(matmul(low(hidden_a), up_w)) + up_b
        active = low(jax.nn.gelu(pre_act, approximate=False))
        ffn_out = low_back(grouped(active, down_w)) + down_b
        hidden_b = layer_norm(hidden_a + ffn_out, gain_b, bias_b)
        embedding = low_back(matmul(low(hidden_b), proj_w)) + proj_b
        return unit_rows(embedding)
    parameters = (tokens.astype(jnp.float32), w_query.astype(jnp.float32), b_query, w_key.astype(jnp.float32), w_value.astype(jnp.float32), b_value, w_out.astype(jnp.float32), b_out, gain_one, bias_one, w_up.astype(jnp.float32), b_up, w_down.astype(jnp.float32), b_down, gain_two, bias_two, w_proj.astype(jnp.float32), b_proj)
    result, pullback = jax.vjp(forward, parameters)
    gradients, = pullback(cotangent.astype(jnp.float32))
    return (result.astype(jnp.bfloat16), gradients[0], gradients[1], gradients[2], gradients[3], gradients[4], gradients[5], gradients[6], gradients[7], gradients[8], gradients[9], gradients[10], gradients[11], gradients[12], gradients[13], gradients[14], gradients[15], gradients[16], gradients[17])
```

```python
import functools

import jax
import jax.numpy as jnp
from jax import lax
from jax.experimental import pallas as pl
from jax.experimental.pallas import tpu as pltpu
from jax.sharding import PartitionSpec as P

HEAD = 64
EPS_NORM = 1e-12
EPS_UNIT = 1e-06
MASKED = -1000000000.0
F32 = jnp.float32
BF16 = jnp.bfloat16
BLK = 256
ANY = pl.ANY


def nn(a, b):
    return lax.dot_general(a, b, (((1,), (0,)), ((), ())), preferred_element_type=F32)


def nt(a, b):
    return lax.dot_general(a, b, (((1,), (1,)), ((), ())), preferred_element_type=F32)


def tn(a, b):
    return lax.dot_general(a, b, (((0,), (0,)), ((), ())), preferred_element_type=F32)


def whole(shape):
    zeros = (0,) * len(shape)
    return pl.BlockSpec(shape, lambda *_: zeros, pipeline_mode=pl.Buffered(1))


def out_whole(shape):
    zeros = (0,) * len(shape)
    return pl.BlockSpec(shape, lambda *_: zeros)


def struct(shape, dtype):
    return jax.ShapeDtypeStruct(shape, dtype)


def call(kernel, name, grid, scalars, in_specs, out_specs, out_shape, scratch, flops, nbytes):
    return pl.pallas_call(
        kernel,
        name=name,
        grid_spec=pltpu.PrefetchScalarGridSpec(
            num_scalar_prefetch=scalars,
            grid=grid,
            in_specs=in_specs,
            out_specs=out_specs,
            scratch_shapes=scratch,
        ),
        out_shape=out_shape,
        cost_estimate=pl.CostEstimate(flops=flops, bytes_accessed=nbytes, transcendentals=0),
        compiler_params=pltpu.CompilerParams(vmem_limit_bytes=60 * 1024 * 1024),
    )


def pair_lanes(head):
    lane = lax.broadcasted_iota(jnp.int32, (1, 128), 1)
    return (lane < HEAD) if head == 0 else (lane >= HEAD)


def attend_fwd_kernel(n_pairs, first, meta, lens, x0, x1, wq, wk, wv, bq, bv, wo, *rest):
    q_out, k_out, v_out, c_out, lse_out = rest[:5]
    wcat = rest[-1]
    width = n_pairs * 128
    step = pl.program_id(0)
    passage = step + first

    @pl.when(step == 0)
    def _():
        wcat[:, 0:width] = wq[...]
        wcat[:, width:2 * width] = wk[...]
        wcat[:, 2 * width:3 * width] = wv[...]

    for part, x in ((0, x0), (1, x1)):
        rows = slice(part * BLK, (part + 1) * BLK)
        acc = nn(x[...], wcat[...])
        q_out[rows, :] = ((acc[:, 0:width] + bq[...]).astype(BF16) * jnp.bfloat16(0.125)).astype(BF16)
        k_out[rows, :] = acc[:, width:2 * width].astype(BF16)
        v_out[rows, :] = (acc[:, 2 * width:3 * width] + bv[...]).astype(BF16)
    length = lens[meta[6 + passage]]
    place = lax.broadcasted_iota(jnp.int32, (1, 2 * BLK), 1)
    middle = passage == 1
    place = jnp.where(
        place < BLK,
        place + jnp.where(middle, meta[9], 0),
        place + jnp.where(middle, meta[10] - BLK, 0),
    )
    bias = jnp.where(place < length, 0.0, MASKED)

    head_lane = lax.broadcasted_iota(jnp.int32, (1, 128), 1)
    stats = jnp.zeros((2 * BLK, 128), F32)
    for pair in range(n_pairs):
        cols = slice(pair * 128, (pair + 1) * 128)
        qp, kp, vp = q_out[:, cols], k_out[:, cols], v_out[:, cols]
        mixed = None
        for head in range(2):
            lanes = pair_lanes(head)
            scores = nt(jnp.where(lanes, qp, jnp.zeros_like(qp)), kp) + bias
            top = jnp.max(scores, axis=-1, keepdims=True)
            shifted = jnp.exp(scores - top)
            total = jnp.sum(shifted, axis=-1, keepdims=True)
            part = nn(shifted.astype(BF16), vp) * (1.0 / total)
            mixed = part if head == 0 else jnp.where(lanes, part, mixed)
            stats = jnp.where(head_lane == 2 * pair + head, top + jnp.log(total), stats)
        c_out[:, cols] = mixed.astype(BF16)
    lse_out[0] = jnp.transpose(stats)[0:8, :]
    if first == 0:
        send, keep = rest[5:7]

        @pl.when(step == 0)
        def _():
            send[BLK:3 * BLK, :] = nn(c_out[...], wo[...]).astype(BF16)

        @pl.when(step == 1)
        def _():
            keep[...] = nn(c_out[0:BLK, :], wo[...]).astype(BF16)
            send[0:BLK, :] = nn(c_out[BLK:2 * BLK, :], wo[...]).astype(BF16)
    else:
        rest[5][...] = nn(c_out[...], wo[...]).astype(BF16)


def attend_fwd(first, steps, meta, lens, tokens, wq, wk, wv, bq, bv, wo):
    d, width = wq.shape
    n_pairs = width // 128
    seq = 2 * BLK
    rows = steps * seq

    def x_map(part):
        return lambda i, meta, lens: (meta[2 * (i + first) + part], 0)

    blk = pl.BlockSpec((seq, width), lambda i, *_: (i, 0))
    outs = [struct((rows, width), BF16)] * 4 + [struct((steps, 8, seq), F32)]
    specs = [blk] * 4 + [pl.BlockSpec((1, 8, seq), lambda i, *_: (i, 0, 0))]
    if first == 0:
        outs += [struct((3 * BLK, d), BF16), struct((BLK, d), BF16)]
        specs += [out_whole((3 * BLK, d)), out_whole((BLK, d))]
    else:
        outs += [struct((seq, d), BF16)]
        specs += [out_whole((seq, d))]
    return call(
        functools.partial(attend_fwd_kernel, n_pairs, first),
        f"attend_fwd_{first}",
        (steps,),
        2,
        [
            pl.BlockSpec((BLK, d), x_map(0)),
            pl.BlockSpec((BLK, d), x_map(1)),
            whole(wq.shape), whole(wk.shape), whole(wv.shape),
            whole((1, width)), whole((1, width)), whole(wo.shape),
        ],
        specs,
        outs,
        [pltpu.VMEM((d, 3 * width), BF16)],
        8 * rows * d * width + 8 * rows * seq * width,
        4 * rows * d + 8 * d * width + 10 * rows * width,
    )(meta, lens, tokens, tokens, wq, wk, wv, bq.reshape(1, -1), bv.reshape(1, -1), wo)


def phi_pair(u):
    size = jnp.abs(u)
    t = 1.0 / (1.0 + (0.3275911 * 0.7071067811865476) * size)
    e = jnp.exp(u * u * (-0.5))
    poly = t * (0.127414796 + t * (-0.142248368 + t * (0.7107068705 + t * (-0.7265760135 + t * 0.5307027145))))
    tail = poly * e
    phi = jnp.where(u >= 0, 1.0 - tail, tail)
    return u * phi, phi + u * (e * 0.3989422804014327)


def ffn_fwd_kernel(
    meta, tok, keep_a, keep_b, recv, cot, wup_o, wup_r, wdn_o, wdn_r, bup_o, bup_r, wproj, vecs, bproj,
    active, slope, hlow, xhat_one, rstd_one, dlow, emb_out, gproj, sums, psum,
    wup, wdn, h_one, acc, pre, rstd_two, gtwo, hfin, acc8, gp_acc, sems,
):
    step = pl.program_id(0)
    d = tok.shape[1]
    half = wup_o.shape[1]
    copies = (
        pltpu.make_async_copy(wup_o, wup.at[0], sems.at[0]),
        pltpu.make_async_copy(wup_r, wup.at[1], sems.at[1]),
        pltpu.make_async_copy(wdn_o, wdn.at[0], sems.at[2]),
        pltpu.make_async_copy(wdn_r, wdn.at[1], sems.at[3]),
    )

    @pl.when(step == 0)
    def _():
        for item in (0, 2, 1, 3):
            copies[item].start()
        acc8[...] = jnp.zeros_like(acc8)
        gp_acc[...] = jnp.zeros_like(gp_acc)
        psum[...] = jnp.zeros_like(psum)

    chunk = 32
    first = step == 0

    @pl.loop(0, BLK // chunk)
    def _(it):
        rows = pl.ds(pl.multiple_of(it * chunk, chunk), chunk)
        mine = jnp.where(first, keep_a[rows, :].astype(F32), keep_b[rows, :].astype(F32))
        r = tok[rows, :].astype(F32) + (mine + recv[rows, :].astype(F32)) + vecs[0:1, :]
        center = r - jnp.mean(r, axis=-1, keepdims=True)
        rstd = lax.rsqrt(jnp.mean(center * center, axis=-1, keepdims=True) + EPS_NORM)
        xhat = center * rstd
        h = xhat * vecs[1:2, :] + vecs[2:3, :]
        h_one[rows, :] = h
        hlow[rows, :] = h.astype(BF16)
        xhat_one[rows, :] = xhat.astype(BF16)
        rstd_one[rows, :] = jnp.broadcast_to(rstd, (chunk, 128))

    tile = 512
    per = half // tile
    n_tiles = 2 * per

    def up(j, slot):
        who, col = j // per, (j % per) * tile
        if per and j % per == 0:
            @pl.when(first)
            def _():
                copies[who].wait()
        pre[slot] = nn(hlow[...], wup[who, :, col:col + tile])

    def act(j, slot):
        who, col = j // per, (j % per) * tile
        bias = (bup_o, bup_r)[who][:, col:col + tile]
        out = j * tile
        for r in range(0, BLK, 16):
            value, grad = phi_pair(pre[slot, r:r + 16, :] + bias)
            active[r:r + 16, out:out + tile] = value.astype(BF16)
            slope[r:r + 16, out:out + tile] = grad.astype(BF16)

    def down(j):
        who, row = j // per, (j % per) * tile
        if j % per == 0:
            @pl.when(first)
            def _():
                copies[2 + who].wait()
        part = nn(active[:, j * tile:(j + 1) * tile], wdn[who, row:row + tile, :])
        if j == 0:
            acc[...] = part
        else:
            acc[...] += part

    up(0, 0)
    for j in range(n_tiles):
        if j + 1 < n_tiles:
            up(j + 1, (j + 1) % 2)
        act(j, j % 2)
        down(j)

    @pl.loop(0, BLK // chunk)
    def _(it):
        rows = pl.ds(pl.multiple_of(it * chunk, chunk), chunk)
        r = h_one[rows, :] + acc[rows, :] + vecs[3:4, :]
        center = r - jnp.mean(r, axis=-1, keepdims=True)
        rstd = lax.rsqrt(jnp.mean(center * center, axis=-1, keepdims=True) + EPS_NORM)
        xhat = center * rstd
        acc[rows, :] = xhat
        rstd_two[rows, :] = jnp.broadcast_to(rstd, (chunk, 128))
        hfin[rows, :] = (xhat * vecs[4:5, :] + vecs[5:6, :]).astype(BF16)

    emb = nn(hfin[...], wproj[...]) + bproj[...]
    norm = lax.rsqrt(jnp.sum(emb * emb, axis=-1, keepdims=True) + EPS_UNIT)
    unit = emb * norm
    emb_out[...] = unit.astype(BF16)
    c = cot[...].astype(F32)
    ge = norm * (c - unit * jnp.sum(unit * c, axis=-1, keepdims=True))
    psum[...] += jnp.sum(ge.reshape(BLK // 8, 8, 128), axis=0)
    gelow = ge.astype(BF16)
    gp_acc[...] += tn(gelow, hfin[...])
    gtwo[...] = nt(gelow, wproj[...])

    @pl.loop(0, BLK // chunk)
    def _(it):
        rows = pl.ds(pl.multiple_of(it * chunk, chunk), chunk)
        dy = gtwo[rows, :]
        xhat = acc[rows, :]
        dz = dy * vecs[4:5, :]
        m_one = jnp.mean(dz, axis=-1, keepdims=True)
        m_two = jnp.mean(dz * xhat, axis=-1, keepdims=True)
        gr = (dz - m_one - xhat * m_two) * rstd_two[rows, 0:1]
        dlow[rows, :] = gr.astype(BF16)
        acc8[0] += jnp.sum(gr.reshape(chunk // 8, 8, d), axis=0)
        acc8[1] += jnp.sum((dy * xhat).reshape(chunk // 8, 8, d), axis=0)
        acc8[2] += jnp.sum(dy.reshape(chunk // 8, 8, d), axis=0)

    @pl.when(step == pl.num_programs(0) - 1)
    def _():
        gproj[...] = gp_acc[...].astype(BF16)
        for row in range(3):
            sums[row:row + 1, :] = jnp.sum(acc8[row], axis=0, keepdims=True)
        sums[3:8, :] = jnp.zeros((5, d), F32)


def ffn_fwd(meta, tokens, keep_a, keep_b, recv, cot, wup_o, wup_r, wdn_o, wdn_r, bup_o, bup_r, wproj, vecs, bproj):
    d, half = wup_o.shape
    rows = 3 * BLK
    proj = wproj.shape[1]
    row_map = lambda i, meta: (i, 0)
    tok_map = lambda i, meta: (meta[jnp.where(i == 0, 2, 3 + i)], 0)
    any_spec = pl.BlockSpec(memory_space=ANY)
    return call(
        ffn_fwd_kernel,
        "ffn_fwd",
        (3,),
        1,
        [
            pl.BlockSpec((BLK, d), tok_map),
            whole((BLK, d)),
            pl.BlockSpec((BLK, d), lambda i, meta: (jnp.maximum(i - 1, 0), 0)),
            pl.BlockSpec((BLK, d), row_map),
            pl.BlockSpec((BLK, proj), tok_map),
            any_spec, any_spec, any_spec, any_spec,
            whole((1, half)), whole((1, half)),
            whole(wproj.shape), whole((8, d)), whole((1, proj)),
        ],
        [
            pl.BlockSpec((BLK, 2 * half), row_map),
            pl.BlockSpec((BLK, 2 * half), row_map),
            pl.BlockSpec((BLK, d), row_map),
            pl.BlockSpec((BLK, d), row_map),
            pl.BlockSpec((BLK, 128), row_map),
            pl.BlockSpec((BLK, d), row_map),
            pl.BlockSpec((BLK, proj), row_map),
            out_whole((proj, d)),
            out_whole((8, d)),
            out_whole((8, proj)),
        ],
        [
            struct((rows, 2 * half), BF16),
            struct((rows, 2 * half), BF16),
            struct((rows, d), BF16),
            struct((rows, d), BF16),
            struct((rows, 128), F32),
            struct((rows, d), BF16),
            struct((rows, proj), BF16),
            struct((proj, d), BF16),
            struct((8, d), F32),
            struct((8, proj), F32),
        ],
        [
            pltpu.VMEM((2, d, half), BF16),
            pltpu.VMEM((2, half, d), BF16),
            pltpu.VMEM((BLK, d), F32),
            pltpu.VMEM((BLK, d), F32),
            pltpu.VMEM((2, BLK, 512), F32),
            pltpu.VMEM((BLK, 128), F32),
            pltpu.VMEM((BLK, d), F32),
            pltpu.VMEM((BLK, d), BF16),
            pltpu.VMEM((3, 8, d), F32),
            pltpu.VMEM((proj, d), F32),
            pltpu.SemaphoreType.DMA((4,)),
        ],
        8 * rows * d * half + 6 * rows * d * proj,
        8 * d * half + 8 * rows * half + 12 * rows * d,
    )(
        meta, tokens, keep_a, keep_b, recv, cot, wup_o, wup_r, wdn_o, wdn_r,
        bup_o.reshape(1, -1), bup_r.reshape(1, -1), wproj, vecs, bproj.reshape(1, -1),
    )


def down_other_kernel(act, dlow, out):
    out[...] = tn(act[...], dlow[...]).astype(BF16)


def down_other(active, dlow):
    rows, d = dlow.shape
    half = active.shape[1] // 2
    tile = 256
    shift = half // tile
    return call(
        down_other_kernel,
        "grad_down_other",
        (half // tile,),
        0,
        [pl.BlockSpec((rows, tile), lambda i: (0, shift + i)), whole((rows, d))],
        pl.BlockSpec((tile, d), lambda i: (i, 0)),
        struct((half, d), BF16),
        [],
        2 * rows * d * half,
        2 * rows * half + 2 * rows * d + 2 * half * d,
    )(active, dlow)


def spread(source, me, shards, rows, outs, at=0):
    middle = shards // 2
    for place in range(shards):
        start = pl.multiple_of(jnp.bitwise_xor(place, me) * rows, 8)
        target = outs[place // middle]
        target[place % middle, at:at + rows, :] = source[pl.ds(start, rows), :].astype(BF16)


def down_own_kernel(shards, ids, act, dlow, recv, gproj, grecv, keep_a, send_a, keep_b, send_b, full, extra):
    step = pl.program_id(0)
    tile = act.shape[1]
    rows = pl.ds(pl.multiple_of(step * tile, tile), tile)
    full[rows, :] = (tn(act[...], dlow[...]) + recv[...].astype(F32)).astype(BF16)

    @pl.when(step == pl.num_programs(0) - 1)
    def _():
        part = full.shape[0] // 2
        per = part // shards
        spread(full.at[0:part], ids[0], shards, per, (keep_a, send_a))
        extra[...] = gproj[...].astype(F32) + grecv[...].astype(F32)
        spread(extra, ids[0], shards, extra.shape[0] // shards, (keep_a, send_a), at=per)
        spread(full.at[part:2 * part], ids[1], shards, per, (keep_b, send_b))


def down_own(shards, ids, active, dlow, recv, gproj, grecv):
    rows, d = dlow.shape
    half = active.shape[1] // 2
    tile = 256
    per = half // 2 // shards
    extra = gproj.shape[0] // shards
    shape_a, shape_b = (shards // 2, per + extra, d), (shards // 2, per, d)
    return call(
        functools.partial(down_own_kernel, shards),
        "grad_down_own",
        (half // tile,),
        1,
        [
            pl.BlockSpec((rows, tile), lambda i, ids: (0, i)),
            whole((rows, d)),
            pl.BlockSpec((tile, d), lambda i, ids: (i, 0)),
            whole(gproj.shape),
            whole(gproj.shape),
        ],
        [out_whole(shape_a)] * 2 + [out_whole(shape_b)] * 2,
        [struct(shape_a, BF16)] * 2 + [struct(shape_b, BF16)] * 2,
        [pltpu.VMEM((half, d), BF16), pltpu.VMEM(gproj.shape, F32)],
        2 * rows * d * half,
        2 * rows * half + 2 * rows * d + 4 * half * d,
    )(ids, active, dlow, recv, gproj, grecv)


def pre_kernel(n_own, dlow, wd_o, wd_r, slope, pre, sums):
    step = pl.program_id(0)

    def run(weight):
        grad = nt(dlow[...], weight[...]) * slope[...].astype(F32)
        sums[...] = jnp.sum(grad.reshape(grad.shape[0] // 8, 8, grad.shape[1]), axis=0)
        pre[...] = grad.astype(BF16)

    @pl.when(step < n_own)
    def _():
        run(wd_o)

    @pl.when(step >= n_own)
    def _():
        run(wd_r)


def grad_pre(dlow, wd_o, wd_r, slope):
    rows, d = dlow.shape
    half = wd_o.shape[0]
    tile = 256
    n_own = half // tile
    return call(
        functools.partial(pre_kernel, n_own),
        "grad_pre",
        (2 * n_own,),
        0,
        [
            whole((rows, d)),
            pl.BlockSpec((tile, d), lambda i: (jnp.minimum(i, n_own - 1), 0)),
            pl.BlockSpec((tile, d), lambda i: (jnp.maximum(i - n_own, 0), 0)),
            pl.BlockSpec((rows, tile), lambda i: (0, i)),
        ],
        [pl.BlockSpec((rows, tile), lambda i: (0, i)), pl.BlockSpec((8, tile), lambda i: (0, i))],
        [struct((rows, 2 * half), BF16), struct((8, 2 * half), F32)],
        [],
        4 * rows * d * half,
        4 * d * half + 8 * rows * half + 2 * rows * d,
    )(dlow, wd_o, wd_r, slope)


def up_other_kernel(hlow, pre, out, flipped):
    @pl.when(pl.program_id(0) == 0)
    def _():
        flipped[...] = jnp.transpose(hlow[...])

    out[...] = nn(flipped[...], pre[...]).astype(BF16)


def up_other(hlow, pre):
    rows, d = hlow.shape
    half = pre.shape[1] // 2
    tile = 512
    shift = half // tile
    return call(
        up_other_kernel,
        "grad_up_other",
        (half // tile,),
        0,
        [whole((rows, d)), pl.BlockSpec((rows, tile), lambda i: (0, shift + i))],
        pl.BlockSpec((d, tile), lambda i: (0, i)),
        struct((d, half), BF16),
        [pltpu.VMEM((d, rows), BF16)],
        2 * rows * d * half,
        2 * rows * half + 2 * rows * d + 2 * half * d,
    )(hlow, pre)


def up_own_kernel(shards, ids, hlow, pre, recv, keep_a, send_a, keep_b, send_b, flipped, full):
    step = pl.program_id(0)
    d = hlow.shape[1]
    tile = pre.shape[1]
    per = d // shards

    @pl.when(step == 0)
    def _():
        flipped[...] = jnp.transpose(hlow[...])

    out = (nn(flipped[...], pre[...]) + recv[...].astype(F32)).astype(BF16)
    full[...] = out
    steps = pl.num_programs(0) // 2
    for part, outs in ((0, (keep_a, send_a)), (1, (keep_b, send_b))):
        for place in range(2):
            @pl.when(step == part * 2 + place)
            def _(part=part, outs=outs, place=place):
                for j in range(shards):
                    start = pl.multiple_of(jnp.bitwise_xor(j, ids[part]) * per, 8)
                    outs[j // (shards // 2)][j % (shards // 2), :, place * tile:(place + 1) * tile] = full[
                        pl.ds(start, per), :
                    ]


def up_own(shards, ids, hlow, pre, recv):
    rows, d = hlow.shape
    half = pre.shape[1] // 2
    tile = half // 4
    shape = (shards // 2, d // shards, half // 2)
    return call(
        functools.partial(up_own_kernel, shards),
        "grad_up_own",
        (4,),
        1,
        [
            whole((rows, d)),
            pl.BlockSpec((rows, tile), lambda i, ids: (0, i)),
            pl.BlockSpec((d, tile), lambda i, ids: (0, i)),
        ],
        [out_whole(shape)] * 4,
        [struct(shape, BF16)] * 4,
        [pltpu.VMEM((d, rows), BF16), pltpu.VMEM((d, tile), BF16)],
        2 * rows * d * half,
        2 * rows * half + 2 * rows * d + 4 * half * d,
    )(ids, hlow, pre, recv)


def hone_kernel(pre, wu_o, wu_r, dlow, xhat_one, rstd_one, gain, mix, sums, grad, acc8):
    step = pl.program_id(0)
    d = dlow.shape[1]
    half = wu_o.shape[1]

    @pl.when(step == 0)
    def _():
        acc8[...] = jnp.zeros_like(acc8)

    grad[...] = nt(pre[:, 0:half], wu_o[...]) + nt(pre[:, half:2 * half], wu_r[...])
    chunk = 32

    @pl.loop(0, BLK // chunk)
    def _(it):
        rows = pl.ds(pl.multiple_of(it * chunk, chunk), chunk)
        dy = grad[rows, :] + dlow[rows, :].astype(F32)
        xhat = xhat_one[rows, :].astype(F32)
        dz = dy * gain[...]
        m_one = jnp.mean(dz, axis=-1, keepdims=True)
        m_two = jnp.mean(dz * xhat, axis=-1, keepdims=True)
        gr = (dz - m_one - xhat * m_two) * rstd_one[rows, 0:1]
        mix[rows, :] = gr.astype(BF16)
        acc8[0] += jnp.sum(gr.reshape(chunk // 8, 8, d), axis=0)
        acc8[1] += jnp.sum((dy * xhat).reshape(chunk // 8, 8, d), axis=0)
        acc8[2] += jnp.sum(dy.reshape(chunk // 8, 8, d), axis=0)

    @pl.when(step == pl.num_programs(0) - 1)
    def _():
        for row in range(3):
            sums[row:row + 1, :] = jnp.sum(acc8[row], axis=0, keepdims=True)
        sums[3:8, :] = jnp.zeros((5, d), F32)


def grad_hone(pre, wu_o, wu_r, dlow, xhat_one, rstd_one, gain):
    rows, d = dlow.shape
    half = wu_o.shape[1]
    blk = lambda n: pl.BlockSpec((BLK, n), lambda i: (i, 0))
    return call(
        hone_kernel,
        "grad_hone",
        (rows // BLK,),
        0,
        [blk(2 * half), whole((d, half)), whole((d, half)), blk(d), blk(d), blk(128), whole((1, d))],
        [blk(d), out_whole((8, d))],
        [struct((rows, d), BF16), struct((8, d), F32)],
        [pltpu.VMEM((BLK, d), F32), pltpu.VMEM((3, 8, d), F32)],
        4 * rows * d * half,
        4 * d * half + 4 * rows * half + 8 * rows * d,
    )(pre, wu_o, wu_r, dlow, xhat_one, rstd_one, gain.reshape(1, -1))


def attend_bwd_kernel(n_pairs, passage, meta, lens, q, k, v, ctx, lse, mix0, mix1, wq, wk, wv, wo, *rest):
    dqkv, dx, sums, gctx, wcat, deltas, lser = rest
    width = n_pairs * 128
    seq = 2 * BLK
    wcat[:, 0:width] = wq[...]
    wcat[:, width:2 * width] = wk[...]
    wcat[:, 2 * width:3 * width] = wv[...]
    for part, mix in ((0, mix0), (1, mix1)):
        gctx[part * BLK:(part + 1) * BLK, :] = nt(mix[...], wo[...]).astype(BF16)
    length = lens[meta[6 + passage]]
    place = lax.broadcasted_iota(jnp.int32, (seq, 1), 0)
    if passage == 1:
        place = jnp.where(place < BLK, place + meta[9], place + meta[10] - BLK)
    bias = jnp.where(place < length, 0.0, MASKED)
    both = gctx[...].astype(F32) * ctx[...].astype(F32)
    high = both.astype(BF16)
    low = (both - high.astype(F32)).astype(BF16)
    owner = lax.broadcasted_iota(jnp.int32, (16, width), 1) // HEAD
    member = (owner == lax.broadcasted_iota(jnp.int32, (16, width), 0)).astype(F32).astype(BF16)
    deltas[...] = (nt(member, high) + nt(member, low))[0:8, :]
    lser[...] = lse[0]
    for pair in range(n_pairs):
        cols = slice(pair * 128, (pair + 1) * 128)
        qp, kp, vp, gp = q[:, cols], k[:, cols], v[:, cols], gctx[:, cols]
        kflip = jnp.transpose(kp)
        dk = dv = dq = None
        for head in range(2):
            lanes = pair_lanes(head)
            here = 2 * pair + head
            qm = jnp.where(lanes, qp, jnp.zeros_like(qp))
            gm = jnp.where(lanes, gp, jnp.zeros_like(gp))
            probs = jnp.exp(nt(kp, qm) + bias - lser[here:here + 1, :])
            dprobs = nt(vp, gm)
            dscores = (probs * (dprobs - deltas[here:here + 1, :])).astype(BF16)
            dv_part = nn(probs.astype(BF16), gm)
            dk_part = nn(dscores, qm)
            dq_part = nn(kflip, dscores)
            if head == 0:
                dk, dv, dq = dk_part, dv_part, dq_part
            else:
                row = lax.broadcasted_iota(jnp.int32, (128, 1), 0)
                dk, dv, dq = dk + dk_part, dv + dv_part, jnp.where(row < HEAD, dq, dq_part)
        dq = jnp.transpose(dq) * 0.125
        sums[0:1, cols] = jnp.sum(dq, axis=0, keepdims=True)
        sums[1:2, cols] = jnp.sum(dv, axis=0, keepdims=True)
        dqkv[:, cols] = dq.astype(BF16)
        dqkv[:, width + pair * 128:width + (pair + 1) * 128] = dk.astype(BF16)
        dqkv[:, 2 * width + pair * 128:2 * width + (pair + 1) * 128] = dv.astype(BF16)
    sums[2:8, :] = jnp.zeros((6, width), F32)
    for part in range(2):
        rows = slice(part * BLK, (part + 1) * BLK)
        dx[rows, :] = nt(dqkv[rows, :], wcat[...]).astype(BF16)


def attend_bwd(passage, meta, lens, saved, own, recv, wq, wk, wv, wo):
    d, width = wq.shape
    n_pairs = width // 128
    seq = 2 * BLK
    q, k, v, ctx, lse = saved
    at = passage if passage < 2 else 0
    blk = pl.BlockSpec((seq, width), lambda i, *_: (at, 0))
    first, second = [((recv, 1), (recv, 2)), ((own, 0), (recv, 0)), ((own, 1), (own, 2))][passage]

    def mix_spec(index):
        return pl.BlockSpec((BLK, d), lambda i, *_: (index, 0))

    return call(
        functools.partial(attend_bwd_kernel, n_pairs, passage),
        f"attend_bwd_{passage}",
        (1,),
        2,
        [
            blk, blk, blk, blk,
            pl.BlockSpec((1, 8, seq), lambda i, *_: (at, 0, 0)),
            mix_spec(first[1]), mix_spec(second[1]),
            whole(wq.shape), whole(wk.shape), whole(wv.shape), whole(wo.shape),
        ],
        [out_whole((seq, 3 * width)), out_whole((seq, d)), out_whole((8, width))],
        [struct((seq, 3 * width), BF16), struct((seq, d), BF16), struct((8, width), F32)],
        [
            pltpu.VMEM((seq, width), BF16),
            pltpu.VMEM((d, 3 * width), BF16),
            pltpu.VMEM((8, seq), F32),
            pltpu.VMEM((8, seq), F32),
        ],
        8 * seq * d * width + 20 * seq * seq * width,
        8 * d * width + 16 * seq * width + 4 * seq * d,
    )(meta, lens, q, k, v, ctx, lse, first[0], second[0], wq, wk, wv, wo)


def attn_weights_kernel(shards, meta, ids, x0, x1, g0, g1, g2, c0, c1, m0, m1, keep_a, send_a, keep_b, send_b, acc, acc_o, full):
    step = pl.program_id(0)
    width = c0.shape[1]
    d = x0.shape[1]

    def add(x, grads, ctx, mix, rows, first):
        part = tn(x[...], grads[rows, :])
        part_o = tn(ctx[rows, :], mix)
        if first:
            acc[...] = part
            acc_o[...] = part_o
        else:
            acc[...] += part
            acc_o[...] += part_o

    lo, hi = slice(0, BLK), slice(BLK, 2 * BLK)
    blk = lambda ref, i: ref[i * BLK:(i + 1) * BLK, :]
    own, recv = m0, m1

    @pl.when(step == 0)
    def _():
        add(x0, g0, c0, blk(recv, 1), lo, True)
        add(x1, g0, c0, blk(recv, 2), hi, False)

    @pl.when(step == 1)
    def _():
        mid_lo, mid_hi = slice(2 * BLK, 3 * BLK), slice(3 * BLK, 4 * BLK)
        acc[...] += tn(x0[...], g1[lo, :]) + tn(x1[...], g1[hi, :])
        acc_o[...] += tn(c0[mid_lo, :], blk(own, 0)) + tn(c0[mid_hi, :], blk(recv, 0))

    @pl.when(step == 2)
    def _():
        add(x0, g2, c1, blk(own, 1), lo, False)
        add(x1, g2, c1, blk(own, 2), hi, False)
        full[:, 0:2 * width] = acc[:, 0:2 * width].astype(BF16)
        spread(full, ids[0], shards, d // shards, (keep_a, send_a))
        full[:, 0:width] = acc[:, 2 * width:3 * width].astype(BF16)
        full[0:width, width:2 * width] = acc_o[:, 0:width].astype(BF16)
        full[width:2 * width, width:2 * width] = acc_o[:, width:2 * width].astype(BF16)
        spread(full, ids[1], shards, d // shards, (keep_b, send_b))


def attn_weights(shards, meta, ids, tokens, grads, ctx_a, ctx_b, own, recv):
    d = tokens.shape[1]
    width = ctx_a.shape[1]
    seq = 2 * BLK
    shape = (shards // 2, d // shards, 2 * width)
    rows = 3 * seq

    def x_map(part):
        return lambda i, meta, ids: (meta[2 * i + part], 0)

    return call(
        functools.partial(attn_weights_kernel, shards),
        "attn_weights",
        (3,),
        2,
        [
            pl.BlockSpec((BLK, d), x_map(0)),
            pl.BlockSpec((BLK, d), x_map(1)),
            whole((seq, 3 * width)), whole((seq, 3 * width)), whole((seq, 3 * width)),
            whole(ctx_a.shape), whole(ctx_b.shape),
            whole(own.shape), whole(recv.shape),
        ],
        [out_whole(shape)] * 4,
        [struct(shape, BF16)] * 4,
        [pltpu.VMEM((d, 3 * width), F32), pltpu.VMEM((width, d), F32), pltpu.VMEM((d, 2 * width), BF16)],
        8 * rows * d * width,
        4 * rows * d + 8 * rows * width + 8 * d * width,
    )(meta, ids, tokens, tokens, grads[0], grads[1], grads[2], ctx_a, ctx_b, own, recv)


def exchange(value, bit, n_data):
    return lax.ppermute(value, "dp", [(i, i ^ bit) for i in range(n_data)])


def add_low(a, b):
    return (a.astype(F32) + b.astype(F32)).astype(BF16)


def reduce_spread(keep, send, bits, n_data):
    for step, bit in enumerate(bits):
        got = exchange(send, bit, n_data)
        if step + 1 < len(bits):
            half = keep.shape[0] // 2
            keep, send = add_low(keep[:half], got[:half]), add_low(keep[half:], got[half:])
        else:
            return add_low(keep, got)


def gather_spread(mine, bits, n_data):
    have = mine
    for bit in reversed(bits):
        got = exchange(have, bit, n_data)
        if bit == bits[0]:
            return have, got
        have = jnp.concatenate([have, got], axis=0)


def place_id(bits):
    me = lax.axis_index("dp")
    value = 0
    for bit in bits:
        value = value * 2 + jnp.where(jnp.bitwise_and(me, bit) != 0, 1, 0)
    return value


def unpack_kernel(half, columns, ids, *refs):
    n_out = sum(len(c) for c in columns)
    ins, outs = refs[:-n_out], refs[-n_out:]
    shard = pl.program_id(0)
    at = 0
    for part, items in enumerate(columns):
        low, high = ins[2 * part], ins[2 * part + 1]
        place = jnp.bitwise_xor(shard, ids[part])
        for source in (low, high):
            @pl.when((place < half) if source is low else (place >= half))
            def _(source=source, items=items, at=at):
                for number, (rows, cols, lift) in enumerate(items):
                    if lift:
                        outs[at + number][...] = source[0, rows, cols].astype(F32)
                    else:
                        outs[at + number][...] = source[0, rows, cols].astype(F32)
        at += len(items)


def unpack(shards, ids, parts, columns, out_shapes, out_specs, name):
    half = shards // 2

    def low_map(part):
        return lambda s, ids: (jnp.bitwise_and(jnp.bitwise_xor(s, ids[part]), half - 1), 0, 0)

    in_specs, args = [], []
    for part, (have, got) in enumerate(parts):
        for array in (have, got):
            in_specs.append(pl.BlockSpec((1,) + array.shape[1:], low_map(part)))
            args.append(array)
    size = sum(a.size for a in args)
    return call(
        functools.partial(unpack_kernel, half, columns),
        name,
        (shards,),
        1,
        in_specs,
        out_specs,
        out_shapes,
        [],
        size,
        6 * size,
    )(ids, *args)


def sum_all(value, n_data):
    value = value + lax.ppermute(value, "tensor", [(0, 1), (1, 0)])
    bit = 1
    while bit < n_data:
        value = value + exchange(value, bit, n_data)
        bit *= 2
    return value


def finish_kernel(meta, own, other, out):
    mine = meta[11 + pl.program_id(0)]
    @pl.when(mine == 1)
    def _():
        out[...] = own[...].astype(F32)

    @pl.when(mine == 0)
    def _():
        out[...] = other[...].astype(F32)


def finish_tokens(meta, own, other):
    rows, d = own.shape
    spec = pl.BlockSpec((BLK, d), lambda i, meta: (meta[17 + i], 0))
    return call(
        finish_kernel,
        "grad_tokens",
        (2 * rows // BLK,),
        1,
        [spec, spec],
        pl.BlockSpec((BLK, d), lambda i, meta: (i, 0)),
        struct((2 * rows, d), F32),
        [],
        rows * d,
        12 * rows * d,
    )(meta, own, other)


def body(
    tokens, lengths, w_query, b_query, w_key, w_value, b_value, w_out, b_out, gain_one, bias_one,
    w_up, b_up, w_down, b_down, gain_two, bias_two, w_proj, b_proj, cotangent,
):
    n_data = lax.axis_size("dp")
    core = lax.axis_index("tensor")
    d = tokens.shape[1]
    half = w_up.shape[1]
    swap = lambda value: lax.ppermute(value, "tensor", [(0, 1), (1, 0)])
    meta = jnp.array(
        [
            [4, 5, 2, 3, 0, 1, 2, 1, 0, 0, BLK, 1, 1, 1, 0, 0, 0, 1, 2, 0, 0, 1, 2],
            [0, 1, 3, 2, 4, 5, 0, 1, 2, BLK, 0, 0, 0, 0, 1, 1, 1, 1, 2, 0, 0, 1, 2],
        ],
        jnp.int32,
    )[core]

    wup_r, wdn_r, bup_r = swap(w_up), swap(w_down), swap(b_up)
    args = (meta, lengths, tokens, w_query, w_key, w_value, b_query, b_value, w_out)
    *saved_a, part_send, keep_a = attend_fwd(0, 2, *args)
    part_recv = swap(part_send)
    *saved_b, keep_b = attend_fwd(2, 1, *args)
    vecs = jnp.stack([b_out, gain_one, bias_one, b_down, gain_two, bias_two, b_out, b_out])
    (active, slope, hlow, xhat_one, rstd_one, dlow, emb, gproj, sums_two, sums_proj) = ffn_fwd(
        meta, tokens, keep_a, keep_b, part_recv, cotangent, w_up, wup_r, w_down, wdn_r, b_up, bup_r, w_proj, vecs, b_proj
    )
    emb_r = swap(emb)

    if n_data == 16:
        bits_a, bits_b = (1, 4, 2, 8), (2, 4, 1, 8)
    else:
        bits_a = tuple(1 << b for b in range(n_data.bit_length() - 1))
        bits_b = bits_a
    shards = 16
    ids = jnp.stack([place_id(bits_a), place_id(bits_b)]).astype(jnp.int32)
    if n_data != shards:
        ids = jnp.zeros((2,), jnp.int32)

    def reduced(keep, send, bits):
        if n_data != shards:
            return lax.psum(jnp.concatenate([keep, send]), "dp")
        return reduce_spread(keep, send, bits, n_data)

    def gathered(mine, bits):
        if n_data != shards:
            return mine[: shards // 2], mine[shards // 2:]
        return gather_spread(mine, bits, n_data)

    other = down_other(active, dlow)
    other_r, gproj_r = swap(other), swap(gproj)
    pre, sums_up = grad_pre(dlow, w_down, wdn_r, slope)
    keep, send, keep2, send2 = down_own(shards, ids, active, dlow, other_r, gproj, gproj_r)
    down_a, down_b = reduced(keep, send, bits_a), reduced(keep2, send2, bits_b)

    other = up_other(hlow, pre)
    other_r = swap(other)
    mix, sums_one = grad_hone(pre, w_up, wup_r, dlow, xhat_one, rstd_one, gain_one)
    mix_r = swap(mix)
    keep, send, keep2, send2 = up_own(shards, ids, hlow, pre, other_r)
    up_a, up_b = reduced(keep, send, bits_a), reduced(keep2, send2, bits_b)

    weights = (w_query, w_key, w_value, w_out)
    bwd = [
        attend_bwd(s, meta, lengths, saved_a if s < 2 else saved_b, mix, mix_r, *weights) for s in range(3)
    ]
    keep, send, keep2, send2 = attn_weights(
        shards, meta, ids, tokens, [b[0] for b in bwd], saved_a[3], saved_b[3], mix, mix_r
    )
    attn_a, attn_b = reduced(keep, send, bits_a), reduced(keep2, send2, bits_b)

    away = jnp.concatenate([bwd[1][1][BLK:], bwd[0][1]], axis=0)
    home = jnp.concatenate([bwd[1][1][:BLK], bwd[2][1]], axis=0)
    grad_rows = (mix.astype(F32) + home.astype(F32) + swap(away).astype(F32)).astype(BF16)
    grad_tokens = finish_tokens(meta, grad_rows, swap(grad_rows))

    emb_pick = lambda a, b: jnp.where(core == 0, a, b)
    first = emb_pick(jnp.concatenate([emb[BLK:], emb[:BLK]]), jnp.concatenate([emb_r[BLK:], emb_r[:BLK]]))
    embeddings = jnp.concatenate([first, emb_pick(emb_r, emb)])

    up_sums = jnp.sum(sums_up, axis=0)
    qv = bwd[0][2] + bwd[1][2] + bwd[2][2]
    mine_up = jnp.stack([up_sums[:half], up_sums[half:]])
    by_core = jnp.where(core == 0, mine_up, mine_up[::-1])
    width = w_query.shape[1]
    by_core_qv = jnp.where(
        (jnp.arange(2) == core)[:, None, None], qv[None, 0:2, :], jnp.zeros((2, 2, width), F32)
    )
    flat = jnp.concatenate(
        [
            sums_two[0:3].reshape(-1), sums_one[0:3].reshape(-1), jnp.sum(sums_proj, axis=0),
            by_core.reshape(-1), by_core_qv.reshape(-1),
        ]
    )
    size = flat.shape[0]
    flat = sum_all(jnp.pad(flat, (0, -size % 1024)).reshape(8, -1), n_data).reshape(-1)[:size]
    vec = lambda i: flat[i * d:(i + 1) * d]
    at = 6 * d + 128
    g_bproj = flat[6 * d:at]
    g_bup = lax.dynamic_slice(flat, (at + core * half,), (half,))
    qv_all = flat[at + 2 * half:].reshape(2, 2, width)
    g_qv = jnp.where(core == 0, qv_all[0], qv_all[1])

    per = d // shards
    rows = slice(0, per)
    blk = lambda n, f: pl.BlockSpec((per, n), f)
    down_parts = [gathered(down_a, bits_a), gathered(down_b, bits_b)]
    extra = w_proj.shape[1] // shards
    every = slice(None)
    g_down_a, g_proj, g_down_b = unpack(
        shards, ids, down_parts,
        (((rows, every, False), (slice(per, per + extra), every, False)), ((rows, every, False),)),
        [struct((d, d), F32), struct((w_proj.shape[1], d), F32), struct((d, d), F32)],
        [blk(d, lambda s, ids: (s, 0)), pl.BlockSpec((extra, d), lambda s, ids: (s, 0)), blk(d, lambda s, ids: (s, 0))],
        "unpack_down",
    )
    g_down = jnp.concatenate([g_down_a, g_down_b])
    up_parts = [gathered(up_a, bits_a), gathered(up_b, bits_b)]
    g_up_a, g_up_b = unpack(
        shards, ids, up_parts,
        (((rows, every, False),), ((rows, every, False),)),
        [struct((d, half // 2), F32)] * 2,
        [blk(half // 2, lambda s, ids: (s, 0))] * 2,
        "unpack_up",
    )
    g_up = jnp.concatenate([g_up_a, g_up_b], axis=1)
    attn_parts = [gathered(attn_a, bits_a), gathered(attn_b, bits_b)]
    left, right = slice(0, width), slice(width, 2 * width)
    g_query, g_key, g_value, g_out = unpack(
        shards, ids, attn_parts,
        (((rows, left, False), (rows, right, False)), ((rows, left, False), (rows, right, True))),
        [struct((d, width), F32)] * 3 + [struct((width, d), F32)],
        [blk(width, lambda s, ids: (s, 0))] * 3
        + [blk(width, lambda s, ids: (s % (shards // 2), s // (shards // 2)))],
        "unpack_attn",
    )
    return (
        embeddings, grad_tokens, g_query, g_qv[0], g_key, g_value, g_qv[1], g_out,
        vec(3), vec(4), vec(5), g_up, g_bup, g_down, vec(0), vec(1), vec(2), g_proj.T, g_bproj,
    )


def solution(mesh):
    rows, cols, split = P("dp", None), P(None, "tensor"), P("tensor")
    return jax.shard_map(
        body,
        mesh=mesh,
        in_specs=(
            rows, P("dp"), cols, split, cols, cols, split, P("tensor", None), P(), P(), P(),
            cols, split, P("tensor", None), P(), P(), P(), P(), P(), rows,
        ),
        out_specs=(
            rows, rows, cols, split, cols, cols, split, P("tensor", None), P(), P(), P(),
            cols, split, P("tensor", None), P(), P(), P(), P(), P(),
        ),
        check_vma=False,
    )
```

```python
import functools

import jax
import jax.numpy as jnp
from jax import lax
from jax.experimental import pallas as pl
from jax.experimental.pallas import tpu as pltpu
from jax.sharding import PartitionSpec as P

HEAD = 64
EPS_NORM = 1e-12
EPS_UNIT = 1e-06
MASKED = -1000000000.0
F32 = jnp.float32
BF16 = jnp.bfloat16
BLK = 256
ANY = pl.ANY


def nn(a, b):
    return lax.dot_general(a, b, (((1,), (0,)), ((), ())), preferred_element_type=F32)


def nt(a, b):
    return lax.dot_general(a, b, (((1,), (1,)), ((), ())), preferred_element_type=F32)


def tn(a, b):
    return lax.dot_general(a, b, (((0,), (0,)), ((), ())), preferred_element_type=F32)


def whole(shape):
    zeros = (0,) * len(shape)
    return pl.BlockSpec(shape, lambda *_: zeros, pipeline_mode=pl.Buffered(1))


def out_whole(shape):
    zeros = (0,) * len(shape)
    return pl.BlockSpec(shape, lambda *_: zeros)


def struct(shape, dtype):
    return jax.ShapeDtypeStruct(shape, dtype)


def call(kernel, name, grid, scalars, in_specs, out_specs, out_shape, scratch, flops, nbytes, vmem=24):
    return pl.pallas_call(
        kernel,
        name=name,
        grid_spec=pltpu.PrefetchScalarGridSpec(
            num_scalar_prefetch=scalars,
            grid=grid,
            in_specs=in_specs,
            out_specs=out_specs,
            scratch_shapes=scratch,
        ),
        out_shape=out_shape,
        cost_estimate=pl.CostEstimate(flops=flops, bytes_accessed=nbytes, transcendentals=0),
        compiler_params=pltpu.CompilerParams(vmem_limit_bytes=vmem * 1024 * 1024),
    )


def pair_lanes(head):
    lane = lax.broadcasted_iota(jnp.int32, (1, 128), 1)
    return (lane < HEAD) if head == 0 else (lane >= HEAD)


def attend_fwd_kernel(n_pairs, first, meta, lens, x0, x1, wq, wk, wv, bq, bv, wo, *rest):
    q_out, k_out, v_out, c_out, lse_out = rest[:5]
    wcat = rest[-1]
    width = n_pairs * 128
    step = pl.program_id(0)
    passage = step + first

    @pl.when(step == 0)
    def _():
        wcat[:, 0:width] = wq[...]
        wcat[:, width:2 * width] = wk[...]
        wcat[:, 2 * width:3 * width] = wv[...]

    for part, x in ((0, x0), (1, x1)):
        rows = slice(part * BLK, (part + 1) * BLK)
        acc = nn(x[...], wcat[...])
        q_out[rows, :] = ((acc[:, 0:width] + bq[...]).astype(BF16) * jnp.bfloat16(0.125)).astype(BF16)
        k_out[rows, :] = acc[:, width:2 * width].astype(BF16)
        v_out[rows, :] = (acc[:, 2 * width:3 * width] + bv[...]).astype(BF16)
    length = lens[meta[6 + passage]]
    place = lax.broadcasted_iota(jnp.int32, (1, 2 * BLK), 1)
    middle = passage == 1
    place = jnp.where(
        place < BLK,
        place + jnp.where(middle, meta[9], 0),
        place + jnp.where(middle, meta[10] - BLK, 0),
    )
    bias = jnp.where(place < length, 0.0, MASKED)

    head_lane = lax.broadcasted_iota(jnp.int32, (1, 128), 1)
    stats = jnp.zeros((2 * BLK, 128), F32)
    for pair in range(n_pairs):
        cols = slice(pair * 128, (pair + 1) * 128)
        qp, kp, vp = q_out[:, cols], k_out[:, cols], v_out[:, cols]
        mixed = None
        for head in range(2):
            lanes = pair_lanes(head)
            scores = nt(jnp.where(lanes, qp, jnp.zeros_like(qp)), kp) + bias
            top = jnp.max(scores, axis=-1, keepdims=True)
            shifted = jnp.exp(scores - top)
            total = jnp.sum(shifted, axis=-1, keepdims=True)
            part = nn(shifted.astype(BF16), vp) * (1.0 / total)
            mixed = part if head == 0 else jnp.where(lanes, part, mixed)
            stats = jnp.where(head_lane == 2 * pair + head, top + jnp.log(total), stats)
        c_out[:, cols] = mixed.astype(BF16)
    lse_out[0] = jnp.transpose(stats)[0:8, :]
    if first == 0:
        send, keep = rest[5:7]

        @pl.when(step == 0)
        def _():
            send[BLK:3 * BLK, :] = nn(c_out[...], wo[...]).astype(BF16)

        @pl.when(step == 1)
        def _():
            keep[...] = nn(c_out[0:BLK, :], wo[...]).astype(BF16)
            send[0:BLK, :] = nn(c_out[BLK:2 * BLK, :], wo[...]).astype(BF16)
    else:
        rest[5][...] = nn(c_out[...], wo[...]).astype(BF16)


def attend_fwd(first, steps, meta, lens, tokens, wq, wk, wv, bq, bv, wo):
    d, width = wq.shape
    n_pairs = width // 128
    seq = 2 * BLK
    rows = steps * seq

    def x_map(part):
        return lambda i, meta, lens: (meta[2 * (i + first) + part], 0)

    blk = pl.BlockSpec((seq, width), lambda i, *_: (i, 0))
    outs = [struct((rows, width), BF16)] * 4 + [struct((steps, 8, seq), F32)]
    specs = [blk] * 4 + [pl.BlockSpec((1, 8, seq), lambda i, *_: (i, 0, 0))]
    if first == 0:
        outs += [struct((3 * BLK, d), BF16), struct((BLK, d), BF16)]
        specs += [out_whole((3 * BLK, d)), out_whole((BLK, d))]
    else:
        outs += [struct((seq, d), BF16)]
        specs += [out_whole((seq, d))]
    return call(
        functools.partial(attend_fwd_kernel, n_pairs, first),
        f"attend_fwd_{first}",
        (steps,),
        2,
        [
            pl.BlockSpec((BLK, d), x_map(0)),
            pl.BlockSpec((BLK, d), x_map(1)),
            whole(wq.shape), whole(wk.shape), whole(wv.shape),
            whole((1, width)), whole((1, width)), whole(wo.shape),
        ],
        specs,
        outs,
        [pltpu.VMEM((d, 3 * width), BF16)],
        8 * rows * d * width + 8 * rows * seq * width,
        4 * rows * d + 8 * d * width + 10 * rows * width,
    )(meta, lens, tokens, tokens, wq, wk, wv, bq.reshape(1, -1), bv.reshape(1, -1), wo)


def phi_pair(u):
    size = jnp.abs(u)
    t = 1.0 / (1.0 + (0.3275911 * 0.7071067811865476) * size)
    e = jnp.exp(u * u * (-0.5))
    poly = t * (0.127414796 + t * (-0.142248368 + t * (0.7107068705 + t * (-0.7265760135 + t * 0.5307027145))))
    tail = poly * e
    phi = jnp.where(u >= 0, 1.0 - tail, tail)
    return u * phi, phi + u * (e * 0.3989422804014327)


def ffn_fwd_kernel(
    meta, tok, keep_a, keep_b, recv, cot, wup_o, wup_r, wdn_o, wdn_r, bup_o, bup_r, wproj, vecs, bproj,
    active, slope, hlow, xhat_one, rstd_one, dlow, emb_out, gproj, sums, psum,
    wup, wdn, h_one, acc, pre, rstd_two, gtwo, hfin, acc8, gp_acc, sems,
):
    step = pl.program_id(0)
    d = tok.shape[1]
    half = wup_o.shape[1]
    copies = (
        pltpu.make_async_copy(wup_o, wup.at[0], sems.at[0]),
        pltpu.make_async_copy(wup_r, wup.at[1], sems.at[1]),
        pltpu.make_async_copy(wdn_o, wdn.at[0], sems.at[2]),
        pltpu.make_async_copy(wdn_r, wdn.at[1], sems.at[3]),
    )

    @pl.when(step == 0)
    def _():
        for item in (0, 2, 1, 3):
            copies[item].start()
        acc8[...] = jnp.zeros_like(acc8)
        gp_acc[...] = jnp.zeros_like(gp_acc)
        psum[...] = jnp.zeros_like(psum)

    chunk = 32
    first = step == 0

    @pl.loop(0, BLK // chunk, unroll=8)
    def _(it):
        rows = pl.ds(pl.multiple_of(it * chunk, chunk), chunk)
        mine = jnp.where(first, keep_a[rows, :].astype(F32), keep_b[rows, :].astype(F32))
        r = tok[rows, :].astype(F32) + (mine + recv[rows, :].astype(F32)) + vecs[0:1, :]
        center = r - jnp.mean(r, axis=-1, keepdims=True)
        rstd = lax.rsqrt(jnp.mean(center * center, axis=-1, keepdims=True) + EPS_NORM)
        xhat = center * rstd
        h = xhat * vecs[1:2, :] + vecs[2:3, :]
        h_one[rows, :] = h
        hlow[rows, :] = h.astype(BF16)
        xhat_one[rows, :] = xhat.astype(BF16)
        rstd_one[rows, :] = jnp.broadcast_to(rstd, (chunk, 128))

    tile = 512
    per = half // tile
    n_tiles = 2 * per

    def up(j, slot):
        who, col = j // per, (j % per) * tile
        if per and j % per == 0:
            @pl.when(first)
            def _():
                copies[who].wait()
        pre[slot] = nn(hlow[...], wup[who, :, col:col + tile])

    def act(j, slot):
        who, col = j // per, (j % per) * tile
        bias = (bup_o, bup_r)[who][:, col:col + tile]
        out = j * tile
        for r in range(0, BLK, 16):
            value, grad = phi_pair(pre[slot, r:r + 16, :] + bias)
            active[r:r + 16, out:out + tile] = value.astype(BF16)
            slope[r:r + 16, out:out + tile] = grad.astype(BF16)

    def down(j):
        who, row = j // per, (j % per) * tile
        if j % per == 0:
            @pl.when(first)
            def _():
                copies[2 + who].wait()
        part = nn(active[:, j * tile:(j + 1) * tile], wdn[who, row:row + tile, :])
        if j == 0:
            acc[...] = part
        else:
            acc[...] += part

    up(0, 0)
    for j in range(n_tiles):
        if j + 1 < n_tiles:
            up(j + 1, (j + 1) % 2)
        act(j, j % 2)
        down(j)

    @pl.loop(0, BLK // chunk, unroll=8)
    def _(it):
        rows = pl.ds(pl.multiple_of(it * chunk, chunk), chunk)
        r = h_one[rows, :] + acc[rows, :] + vecs[3:4, :]
        center = r - jnp.mean(r, axis=-1, keepdims=True)
        rstd = lax.rsqrt(jnp.mean(center * center, axis=-1, keepdims=True) + EPS_NORM)
        xhat = center * rstd
        acc[rows, :] = xhat
        rstd_two[rows, :] = jnp.broadcast_to(rstd, (chunk, 128))
        hfin[rows, :] = (xhat * vecs[4:5, :] + vecs[5:6, :]).astype(BF16)

    emb = nn(hfin[...], wproj[...]) + bproj[...]
    norm = lax.rsqrt(jnp.sum(emb * emb, axis=-1, keepdims=True) + EPS_UNIT)
    unit = emb * norm
    emb_out[...] = unit.astype(BF16)
    c = cot[...].astype(F32)
    ge = norm * (c - unit * jnp.sum(unit * c, axis=-1, keepdims=True))
    psum[...] += jnp.sum(ge.reshape(BLK // 8, 8, 128), axis=0)
    gelow = ge.astype(BF16)
    gp_acc[...] += tn(gelow, hfin[...])
    gtwo[...] = nt(gelow, wproj[...])

    @pl.loop(0, BLK // chunk, unroll=8)
    def _(it):
        rows = pl.ds(pl.multiple_of(it * chunk, chunk), chunk)
        dy = gtwo[rows, :]
        xhat = acc[rows, :]
        dz = dy * vecs[4:5, :]
        m_one = jnp.mean(dz, axis=-1, keepdims=True)
        m_two = jnp.mean(dz * xhat, axis=-1, keepdims=True)
        gr = (dz - m_one - xhat * m_two) * rstd_two[rows, 0:1]
        dlow[rows, :] = gr.astype(BF16)
        acc8[0] += jnp.sum(gr.reshape(chunk // 8, 8, d), axis=0)
        acc8[1] += jnp.sum((dy * xhat).reshape(chunk // 8, 8, d), axis=0)
        acc8[2] += jnp.sum(dy.reshape(chunk // 8, 8, d), axis=0)

    @pl.when(step == pl.num_programs(0) - 1)
    def _():
        gproj[...] = gp_acc[...].astype(BF16)
        for row in range(3):
            sums[row:row + 1, :] = jnp.sum(acc8[row], axis=0, keepdims=True)
        sums[3:8, :] = jnp.zeros((5, d), F32)


def ffn_fwd(meta, tokens, keep_a, keep_b, recv, cot, wup_o, wup_r, wdn_o, wdn_r, bup_o, bup_r, wproj, vecs, bproj):
    d, half = wup_o.shape
    rows = 3 * BLK
    proj = wproj.shape[1]
    row_map = lambda i, meta: (i, 0)
    tok_map = lambda i, meta: (meta[jnp.where(i == 0, 2, 3 + i)], 0)
    any_spec = pl.BlockSpec(memory_space=ANY)
    return call(
        ffn_fwd_kernel,
        "ffn_fwd",
        (3,),
        1,
        [
            pl.BlockSpec((BLK, d), tok_map),
            whole((BLK, d)),
            pl.BlockSpec((BLK, d), lambda i, meta: (jnp.maximum(i - 1, 0), 0)),
            pl.BlockSpec((BLK, d), row_map),
            pl.BlockSpec((BLK, proj), tok_map),
            any_spec, any_spec, any_spec, any_spec,
            whole((1, half)), whole((1, half)),
            whole(wproj.shape), whole((8, d)), whole((1, proj)),
        ],
        [
            pl.BlockSpec((BLK, 2 * half), row_map),
            pl.BlockSpec((BLK, 2 * half), row_map),
            pl.BlockSpec((BLK, d), row_map),
            pl.BlockSpec((BLK, d), row_map),
            pl.BlockSpec((BLK, 128), row_map),
            pl.BlockSpec((BLK, d), row_map),
            pl.BlockSpec((BLK, proj), row_map),
            out_whole((proj, d)),
            out_whole((8, d)),
            out_whole((8, proj)),
        ],
        [
            struct((rows, 2 * half), BF16),
            struct((rows, 2 * half), BF16),
            struct((rows, d), BF16),
            struct((rows, d), BF16),
            struct((rows, 128), F32),
            struct((rows, d), BF16),
            struct((rows, proj), BF16),
            struct((proj, d), BF16),
            struct((8, d), F32),
            struct((8, proj), F32),
        ],
        [
            pltpu.VMEM((2, d, half), BF16),
            pltpu.VMEM((2, half, d), BF16),
            pltpu.VMEM((BLK, d), F32),
            pltpu.VMEM((BLK, d), F32),
            pltpu.VMEM((2, BLK, 512), F32),
            pltpu.VMEM((BLK, 128), F32),
            pltpu.VMEM((BLK, d), F32),
            pltpu.VMEM((BLK, d), BF16),
            pltpu.VMEM((3, 8, d), F32),
            pltpu.VMEM((proj, d), F32),
            pltpu.SemaphoreType.DMA((4,)),
        ],
        8 * rows * d * half + 6 * rows * d * proj,
        8 * d * half + 8 * rows * half + 12 * rows * d,
    )(
        meta, tokens, keep_a, keep_b, recv, cot, wup_o, wup_r, wdn_o, wdn_r,
        bup_o.reshape(1, -1), bup_r.reshape(1, -1), wproj, vecs, bproj.reshape(1, -1),
    )


def down_other_kernel(act, dlow, out):
    out[...] = tn(act[...], dlow[...]).astype(BF16)


def down_other(active, dlow):
    rows, d = dlow.shape
    half = active.shape[1] // 2
    tile = 256
    shift = half // tile
    return call(
        down_other_kernel,
        "grad_down_other",
        (half // tile,),
        0,
        [pl.BlockSpec((rows, tile), lambda i: (0, shift + i)), whole((rows, d))],
        pl.BlockSpec((tile, d), lambda i: (i, 0)),
        struct((half, d), BF16),
        [],
        2 * rows * d * half,
        2 * rows * half + 2 * rows * d + 2 * half * d,
    )(active, dlow)


def spread(source, me, shards, rows, outs, at=0):
    middle = shards // 2
    for place in range(shards):
        start = pl.multiple_of(jnp.bitwise_xor(place, me) * rows, 8)
        target = outs[place // middle]
        target[place % middle, at:at + rows, :] = source[pl.ds(start, rows), :].astype(BF16)


def down_own_kernel(shards, ids, act, dlow, recv, gproj, grecv, keep_a, send_a, keep_b, send_b, full, extra):
    step = pl.program_id(0)
    tile = act.shape[1]
    rows = pl.ds(pl.multiple_of(step * tile, tile), tile)
    full[rows, :] = (tn(act[...], dlow[...]) + recv[...].astype(F32)).astype(BF16)

    @pl.when(step == pl.num_programs(0) - 1)
    def _():
        part = full.shape[0] // 2
        per = part // shards
        spread(full.at[0:part], ids[0], shards, per, (keep_a, send_a))
        extra[...] = gproj[...].astype(F32) + grecv[...].astype(F32)
        spread(extra, ids[0], shards, extra.shape[0] // shards, (keep_a, send_a), at=per)
        spread(full.at[part:2 * part], ids[1], shards, per, (keep_b, send_b))


def down_own(shards, ids, active, dlow, recv, gproj, grecv):
    rows, d = dlow.shape
    half = active.shape[1] // 2
    tile = 256
    per = half // 2 // shards
    extra = gproj.shape[0] // shards
    shape_a, shape_b = (shards // 2, per + extra, d), (shards // 2, per, d)
    return call(
        functools.partial(down_own_kernel, shards),
        "grad_down_own",
        (half // tile,),
        1,
        [
            pl.BlockSpec((rows, tile), lambda i, ids: (0, i)),
            whole((rows, d)),
            pl.BlockSpec((tile, d), lambda i, ids: (i, 0)),
            whole(gproj.shape),
            whole(gproj.shape),
        ],
        [out_whole(shape_a)] * 2 + [out_whole(shape_b)] * 2,
        [struct(shape_a, BF16)] * 2 + [struct(shape_b, BF16)] * 2,
        [pltpu.VMEM((half, d), BF16), pltpu.VMEM(gproj.shape, F32)],
        2 * rows * d * half,
        2 * rows * half + 2 * rows * d + 4 * half * d,
    )(ids, active, dlow, recv, gproj, grecv)


def pre_kernel(n_own, dlow, wd_o, wd_r, slope, pre, sums):
    step = pl.program_id(0)

    def run(weight):
        grad = nt(dlow[...], weight[...]) * slope[...].astype(F32)
        sums[...] = jnp.sum(grad.reshape(grad.shape[0] // 8, 8, grad.shape[1]), axis=0)
        pre[...] = grad.astype(BF16)

    @pl.when(step < n_own)
    def _():
        run(wd_o)

    @pl.when(step >= n_own)
    def _():
        run(wd_r)


def grad_pre(dlow, wd_o, wd_r, slope):
    rows, d = dlow.shape
    half = wd_o.shape[0]
    tile = 256
    n_own = half // tile
    return call(
        functools.partial(pre_kernel, n_own),
        "grad_pre",
        (2 * n_own,),
        0,
        [
            whole((rows, d)),
            pl.BlockSpec((tile, d), lambda i: (jnp.minimum(i, n_own - 1), 0)),
            pl.BlockSpec((tile, d), lambda i: (jnp.maximum(i - n_own, 0), 0)),
            pl.BlockSpec((rows, tile), lambda i: (0, i)),
        ],
        [pl.BlockSpec((rows, tile), lambda i: (0, i)), pl.BlockSpec((8, tile), lambda i: (0, i))],
        [struct((rows, 2 * half), BF16), struct((8, 2 * half), F32)],
        [],
        4 * rows * d * half,
        4 * d * half + 8 * rows * half + 2 * rows * d,
    )(dlow, wd_o, wd_r, slope)


def up_other_kernel(hlow, pre, out, flipped):
    @pl.when(pl.program_id(0) == 0)
    def _():
        flipped[...] = jnp.transpose(hlow[...])

    out[...] = nn(flipped[...], pre[...]).astype(BF16)


def up_other(hlow, pre):
    rows, d = hlow.shape
    half = pre.shape[1] // 2
    tile = 512
    shift = half // tile
    return call(
        up_other_kernel,
        "grad_up_other",
        (half // tile,),
        0,
        [whole((rows, d)), pl.BlockSpec((rows, tile), lambda i: (0, shift + i))],
        pl.BlockSpec((d, tile), lambda i: (0, i)),
        struct((d, half), BF16),
        [pltpu.VMEM((d, rows), BF16)],
        2 * rows * d * half,
        2 * rows * half + 2 * rows * d + 2 * half * d,
    )(hlow, pre)


def up_own_kernel(shards, ids, hlow, pre, recv, keep_a, send_a, keep_b, send_b, flipped, full):
    step = pl.program_id(0)
    d = hlow.shape[1]
    tile = pre.shape[1]
    per = d // shards

    @pl.when(step == 0)
    def _():
        flipped[...] = jnp.transpose(hlow[...])

    out = (nn(flipped[...], pre[...]) + recv[...].astype(F32)).astype(BF16)
    full[...] = out
    steps = pl.num_programs(0) // 2
    for part, outs in ((0, (keep_a, send_a)), (1, (keep_b, send_b))):
        for place in range(2):
            @pl.when(step == part * 2 + place)
            def _(part=part, outs=outs, place=place):
                for j in range(shards):
                    start = pl.multiple_of(jnp.bitwise_xor(j, ids[part]) * per, 8)
                    outs[j // (shards // 2)][j % (shards // 2), :, place * tile:(place + 1) * tile] = full[
                        pl.ds(start, per), :
                    ]


def up_own(shards, ids, hlow, pre, recv):
    rows, d = hlow.shape
    half = pre.shape[1] // 2
    tile = half // 4
    shape = (shards // 2, d // shards, half // 2)
    return call(
        functools.partial(up_own_kernel, shards),
        "grad_up_own",
        (4,),
        1,
        [
            whole((rows, d)),
            pl.BlockSpec((rows, tile), lambda i, ids: (0, i)),
            pl.BlockSpec((d, tile), lambda i, ids: (0, i)),
        ],
        [out_whole(shape)] * 4,
        [struct(shape, BF16)] * 4,
        [pltpu.VMEM((d, rows), BF16), pltpu.VMEM((d, tile), BF16)],
        2 * rows * d * half,
        2 * rows * half + 2 * rows * d + 4 * half * d,
    )(ids, hlow, pre, recv)


def hone_kernel(pre, wu_o, wu_r, dlow, xhat_one, rstd_one, gain, mix, sums, grad, acc8):
    step = pl.program_id(0)
    d = dlow.shape[1]
    half = wu_o.shape[1]

    @pl.when(step == 0)
    def _():
        acc8[...] = jnp.zeros_like(acc8)

    grad[...] = nt(pre[:, 0:half], wu_o[...]) + nt(pre[:, half:2 * half], wu_r[...])
    chunk = 32

    @pl.loop(0, BLK // chunk, unroll=8)
    def _(it):
        rows = pl.ds(pl.multiple_of(it * chunk, chunk), chunk)
        dy = grad[rows, :] + dlow[rows, :].astype(F32)
        xhat = xhat_one[rows, :].astype(F32)
        dz = dy * gain[...]
        m_one = jnp.mean(dz, axis=-1, keepdims=True)
        m_two = jnp.mean(dz * xhat, axis=-1, keepdims=True)
        gr = (dz - m_one - xhat * m_two) * rstd_one[rows, 0:1]
        mix[rows, :] = gr.astype(BF16)
        acc8[0] += jnp.sum(gr.reshape(chunk // 8, 8, d), axis=0)
        acc8[1] += jnp.sum((dy * xhat).reshape(chunk // 8, 8, d), axis=0)
        acc8[2] += jnp.sum(dy.reshape(chunk // 8, 8, d), axis=0)

    @pl.when(step == pl.num_programs(0) - 1)
    def _():
        for row in range(3):
            sums[row:row + 1, :] = jnp.sum(acc8[row], axis=0, keepdims=True)
        sums[3:8, :] = jnp.zeros((5, d), F32)


def grad_hone(pre, wu_o, wu_r, dlow, xhat_one, rstd_one, gain):
    rows, d = dlow.shape
    half = wu_o.shape[1]
    blk = lambda n: pl.BlockSpec((BLK, n), lambda i: (i, 0))
    return call(
        hone_kernel,
        "grad_hone",
        (rows // BLK,),
        0,
        [blk(2 * half), whole((d, half)), whole((d, half)), blk(d), blk(d), blk(128), whole((1, d))],
        [blk(d), out_whole((8, d))],
        [struct((rows, d), BF16), struct((8, d), F32)],
        [pltpu.VMEM((BLK, d), F32), pltpu.VMEM((3, 8, d), F32)],
        4 * rows * d * half,
        4 * d * half + 4 * rows * half + 8 * rows * d,
    )(pre, wu_o, wu_r, dlow, xhat_one, rstd_one, gain.reshape(1, -1))


def attend_bwd_kernel(n_pairs, passage, meta, lens, q, k, v, ctx, lse, mix0, mix1, wq, wk, wv, wo, *rest):
    dqkv, dx, sums, gctx, wcat, deltas, lser = rest
    width = n_pairs * 128
    seq = 2 * BLK
    wcat[:, 0:width] = wq[...]
    wcat[:, width:2 * width] = wk[...]
    wcat[:, 2 * width:3 * width] = wv[...]
    for part, mix in ((0, mix0), (1, mix1)):
        gctx[part * BLK:(part + 1) * BLK, :] = nt(mix[...], wo[...]).astype(BF16)
    length = lens[meta[6 + passage]]
    place = lax.broadcasted_iota(jnp.int32, (seq, 1), 0)
    if passage == 1:
        place = jnp.where(place < BLK, place + meta[9], place + meta[10] - BLK)
    bias = jnp.where(place < length, 0.0, MASKED)
    both = gctx[...].astype(F32) * ctx[...].astype(F32)
    high = both.astype(BF16)
    low = (both - high.astype(F32)).astype(BF16)
    owner = lax.broadcasted_iota(jnp.int32, (16, width), 1) // HEAD
    member = (owner == lax.broadcasted_iota(jnp.int32, (16, width), 0)).astype(F32).astype(BF16)
    deltas[...] = (nt(member, high) + nt(member, low))[0:8, :]
    lser[...] = lse[0]
    for pair in range(n_pairs):
        cols = slice(pair * 128, (pair + 1) * 128)
        qp, kp, vp, gp = q[:, cols], k[:, cols], v[:, cols], gctx[:, cols]
        kflip = jnp.transpose(kp)
        dk = dv = dq = None
        for head in range(2):
            lanes = pair_lanes(head)
            here = 2 * pair + head
            qm = jnp.where(lanes, qp, jnp.zeros_like(qp))
            gm = jnp.where(lanes, gp, jnp.zeros_like(gp))
            probs = jnp.exp(nt(kp, qm) + bias - lser[here:here + 1, :])
            dprobs = nt(vp, gm)
            dscores = (probs * (dprobs - deltas[here:here + 1, :])).astype(BF16)
            dv_part = nn(probs.astype(BF16), gm)
            dk_part = nn(dscores, qm)
            dq_part = nn(kflip, dscores)
            if head == 0:
                dk, dv, dq = dk_part, dv_part, dq_part
            else:
                row = lax.broadcasted_iota(jnp.int32, (128, 1), 0)
                dk, dv, dq = dk + dk_part, dv + dv_part, jnp.where(row < HEAD, dq, dq_part)
        dq = jnp.transpose(dq) * 0.125
        sums[0:1, cols] = jnp.sum(dq, axis=0, keepdims=True)
        sums[1:2, cols] = jnp.sum(dv, axis=0, keepdims=True)
        dqkv[:, cols] = dq.astype(BF16)
        dqkv[:, width + pair * 128:width + (pair + 1) * 128] = dk.astype(BF16)
        dqkv[:, 2 * width + pair * 128:2 * width + (pair + 1) * 128] = dv.astype(BF16)
    sums[2:8, :] = jnp.zeros((6, width), F32)
    for part in range(2):
        rows = slice(part * BLK, (part + 1) * BLK)
        dx[rows, :] = nt(dqkv[rows, :], wcat[...]).astype(BF16)


def attend_bwd(passage, meta, lens, saved, own, recv, wq, wk, wv, wo):
    d, width = wq.shape
    n_pairs = width // 128
    seq = 2 * BLK
    q, k, v, ctx, lse = saved
    at = passage if passage < 2 else 0
    blk = pl.BlockSpec((seq, width), lambda i, *_: (at, 0))
    first, second = [((recv, 1), (recv, 2)), ((own, 0), (recv, 0)), ((own, 1), (own, 2))][passage]

    def mix_spec(index):
        return pl.BlockSpec((BLK, d), lambda i, *_: (index, 0))

    return call(
        functools.partial(attend_bwd_kernel, n_pairs, passage),
        f"attend_bwd_{passage}",
        (1,),
        2,
        [
            blk, blk, blk, blk,
            pl.BlockSpec((1, 8, seq), lambda i, *_: (at, 0, 0)),
            mix_spec(first[1]), mix_spec(second[1]),
            whole(wq.shape), whole(wk.shape), whole(wv.shape), whole(wo.shape),
        ],
        [out_whole((seq, 3 * width)), out_whole((seq, d)), out_whole((8, width))],
        [struct((seq, 3 * width), BF16), struct((seq, d), BF16), struct((8, width), F32)],
        [
            pltpu.VMEM((seq, width), BF16),
            pltpu.VMEM((d, 3 * width), BF16),
            pltpu.VMEM((8, seq), F32),
            pltpu.VMEM((8, seq), F32),
        ],
        8 * seq * d * width + 20 * seq * seq * width,
        8 * d * width + 16 * seq * width + 4 * seq * d,
    )(meta, lens, q, k, v, ctx, lse, first[0], second[0], wq, wk, wv, wo)


def attn_weights_kernel(shards, meta, ids, x0, x1, g0, g1, g2, c0, c1, m0, m1, keep_a, send_a, keep_b, send_b, acc, acc_o, full):
    step = pl.program_id(0)
    width = c0.shape[1]
    d = x0.shape[1]

    def add(x, grads, ctx, mix, rows, first):
        part = tn(x[...], grads[rows, :])
        part_o = tn(ctx[rows, :], mix)
        if first:
            acc[...] = part
            acc_o[...] = part_o
        else:
            acc[...] += part
            acc_o[...] += part_o

    lo, hi = slice(0, BLK), slice(BLK, 2 * BLK)
    blk = lambda ref, i: ref[i * BLK:(i + 1) * BLK, :]
    own, recv = m0, m1

    @pl.when(step == 0)
    def _():
        add(x0, g0, c0, blk(recv, 1), lo, True)
        add(x1, g0, c0, blk(recv, 2), hi, False)

    @pl.when(step == 1)
    def _():
        mid_lo, mid_hi = slice(2 * BLK, 3 * BLK), slice(3 * BLK, 4 * BLK)
        acc[...] += tn(x0[...], g1[lo, :]) + tn(x1[...], g1[hi, :])
        acc_o[...] += tn(c0[mid_lo, :], blk(own, 0)) + tn(c0[mid_hi, :], blk(recv, 0))

    @pl.when(step == 2)
    def _():
        add(x0, g2, c1, blk(own, 1), lo, False)
        add(x1, g2, c1, blk(own, 2), hi, False)
        full[:, 0:2 * width] = acc[:, 0:2 * width].astype(BF16)
        spread(full, ids[0], shards, d // shards, (keep_a, send_a))
        full[:, 0:width] = acc[:, 2 * width:3 * width].astype(BF16)
        full[0:width, width:2 * width] = acc_o[:, 0:width].astype(BF16)
        full[width:2 * width, width:2 * width] = acc_o[:, width:2 * width].astype(BF16)
        spread(full, ids[1], shards, d // shards, (keep_b, send_b))


def attn_weights(shards, meta, ids, tokens, grads, ctx_a, ctx_b, own, recv):
    d = tokens.shape[1]
    width = ctx_a.shape[1]
    seq = 2 * BLK
    shape = (shards // 2, d // shards, 2 * width)
    rows = 3 * seq

    def x_map(part):
        return lambda i, meta, ids: (meta[2 * i + part], 0)

    return call(
        functools.partial(attn_weights_kernel, shards),
        "attn_weights",
        (3,),
        2,
        [
            pl.BlockSpec((BLK, d), x_map(0)),
            pl.BlockSpec((BLK, d), x_map(1)),
            whole((seq, 3 * width)), whole((seq, 3 * width)), whole((seq, 3 * width)),
            whole(ctx_a.shape), whole(ctx_b.shape),
            whole(own.shape), whole(recv.shape),
        ],
        [out_whole(shape)] * 4,
        [struct(shape, BF16)] * 4,
        [pltpu.VMEM((d, 3 * width), F32), pltpu.VMEM((width, d), F32), pltpu.VMEM((d, 2 * width), BF16)],
        8 * rows * d * width,
        4 * rows * d + 8 * rows * width + 8 * d * width,
    )(meta, ids, tokens, tokens, grads[0], grads[1], grads[2], ctx_a, ctx_b, own, recv)


def after(value, *tokens):
    leaves, tree = jax.tree.flatten(value)
    out = lax.optimization_barrier((*leaves, *tokens))
    return jax.tree.unflatten(tree, out[: len(leaves)])


def exchange(value, bit, n_data):
    return lax.ppermute(value, "dp", [(i, i ^ bit) for i in range(n_data)])


def add_low(a, b):
    return (a.astype(F32) + b.astype(F32)).astype(BF16)


class Chain:
    def __init__(self, parts, orders, n_data):
        self.orders, self.n_data = orders, n_data
        self.hop = 0
        self.keep = [keep for keep, _ in parts]
        self.send([send for _, send in parts])

    def bit(self, part):
        order = self.orders[part]
        return (order + order[::-1])[self.hop]

    def send(self, values):
        self.token = values[-1]
        self.got = [exchange(value, self.bit(i), self.n_data) for i, value in enumerate(values)]
        self.hop += 1

    def advance(self, *tokens):
        self.keep, self.got = after((self.keep, self.got), *tokens)
        hops = len(self.orders[0])
        if self.hop < hops:
            half = [keep.shape[0] // 2 for keep in self.keep]
            sends = [add_low(k[h:], g[h:]) for k, g, h in zip(self.keep, self.got, half)]
            self.keep = [add_low(k[:h], g[:h]) for k, g, h in zip(self.keep, self.got, half)]
            self.send(sends)
        elif self.hop == hops:
            self.keep = [add_low(k, g) for k, g in zip(self.keep, self.got)]
            self.send(self.keep)
        elif self.hop < 2 * hops:
            self.keep = [jnp.concatenate([k, g]) for k, g in zip(self.keep, self.got)]
            self.send(self.keep)
        return self.token

    def result(self):
        return list(zip(self.keep, self.got))


class Plain:
    def __init__(self, parts):
        sums = [lax.psum(jnp.concatenate(part), "dp") for part in parts]
        self.pairs = [(total[: total.shape[0] // 2], total[total.shape[0] // 2:]) for total in sums]
        self.token = sums[-1]

    def advance(self, *tokens):
        return self.token

    def result(self):
        return self.pairs


def place_id(bits):
    me = lax.axis_index("dp")
    value = 0
    for bit in bits:
        value = value * 2 + jnp.where(jnp.bitwise_and(me, bit) != 0, 1, 0)
    return value


def picked(low, high, place, half, rows):
    at = jnp.bitwise_and(place, half - 1)
    return jnp.where(place < half, low[at, rows, :].astype(F32), high[at, rows, :].astype(F32))


def unpack_down_kernel(shards, per, ids, low_a, high_a, low_b, high_b, out, extra):
    step = pl.program_id(0)
    half, group = shards // 2, shards // 4
    more = low_a.shape[1] - per
    for part, (low, high) in enumerate(((low_a, high_a), (low_b, high_b))):
        @pl.when(step // 4 == part)
        def _(part=part, low=low, high=high):
            for q in range(group):
                shard = (step % 4) * group + q
                place = jnp.bitwise_xor(shard, ids[part])
                out[q * per:(q + 1) * per, :] = picked(low, high, place, half, slice(0, per))
                if part == 0:
                    rows = pl.ds(pl.multiple_of(shard * more, more), more)
                    extra[rows, :] = picked(low, high, place, half, slice(per, per + more))


def unpack_down(shards, ids, parts):
    args = [array for part in parts for array in part]
    d = args[0].shape[2]
    per = args[2].shape[1]
    more = args[0].shape[1] - per
    rows = 2 * shards * per
    return call(
        functools.partial(unpack_down_kernel, shards, per),
        "unpack_down",
        (8,),
        1,
        [whole(array.shape) for array in args],
        [pl.BlockSpec((rows // 8, d), lambda i, ids: (i, 0)), out_whole((shards * more, d))],
        [struct((rows, d), F32), struct((shards * more, d), F32)],
        [],
        rows * d,
        6 * rows * d,
    )(ids, *args)


def unpack_up_kernel(shards, ids, low_a, high_a, low_b, high_b, out):
    step = pl.program_id(0)
    half, group = shards // 2, shards // 4
    per, wide = low_a.shape[1:]
    for part, (low, high) in enumerate(((low_a, high_a), (low_b, high_b))):
        for q in range(group):
            place = jnp.bitwise_xor(step * group + q, ids[part])
            out[q * per:(q + 1) * per, part * wide:(part + 1) * wide] = picked(low, high, place, half, slice(None))


def unpack_up(shards, ids, parts):
    args = [array for part in parts for array in part]
    per, wide = args[0].shape[1:]
    rows = shards * per
    return call(
        functools.partial(unpack_up_kernel, shards),
        "unpack_up",
        (4,),
        1,
        [whole(array.shape) for array in args],
        pl.BlockSpec((rows // 4, 2 * wide), lambda i, ids: (i, 0)),
        struct((rows, 2 * wide), F32),
        [],
        2 * rows * wide,
        12 * rows * wide,
    )(ids, *args)


def unpack_attn_kernel(shards, ids, low_a, high_a, low_b, high_b, query, key, value, out):
    step = pl.program_id(0)
    half, group = shards // 2, shards // 4
    per, wide = low_a.shape[1:]
    width = wide // 2
    every = slice(None)
    for q in range(group):
        shard = step * group + q
        rows = slice(q * per, (q + 1) * per)
        both = picked(low_a, high_a, jnp.bitwise_xor(shard, ids[0]), half, every)
        query[rows, :], key[rows, :] = both[:, :width], both[:, width:]
        value[rows, :] = picked(low_b, high_b, jnp.bitwise_xor(shard, ids[1]), half, every)[:, :width]
    for q in range(group // 2):
        rows = slice(q * per, (q + 1) * per)
        for side in range(2):
            shard = step * (group // 2) + q + side * half
            both = picked(low_b, high_b, jnp.bitwise_xor(shard, ids[1]), half, every)
            out[rows, side * width:(side + 1) * width] = both[:, width:]


def unpack_attn(shards, ids, parts):
    args = [array for part in parts for array in part]
    per, wide = args[0].shape[1:]
    rows, width = shards * per, wide // 2
    spec = pl.BlockSpec((rows // 4, width), lambda i, ids: (i, 0))
    return call(
        functools.partial(unpack_attn_kernel, shards),
        "unpack_attn",
        (4,),
        1,
        [whole(array.shape) for array in args],
        [spec, spec, spec, pl.BlockSpec((width // 4, rows), lambda i, ids: (i, 0))],
        [struct((rows, width), F32)] * 3 + [struct((width, rows), F32)],
        [],
        2 * rows * wide,
        12 * rows * wide,
    )(ids, *args)


def finish_kernel(meta, own, other, out):
    step = pl.program_id(0)
    rows = pl.ds(pl.multiple_of(meta[17 + step] * BLK, BLK), BLK)
    out[...] = jnp.where(meta[11 + step] == 1, own[rows, :].astype(F32), other[rows, :].astype(F32))


def finish_tokens(meta, own, other):
    rows, d = own.shape
    return call(
        finish_kernel,
        "grad_tokens",
        (2 * rows // BLK,),
        1,
        [whole((rows, d)), whole((rows, d))],
        pl.BlockSpec((BLK, d), lambda i, meta: (i, 0)),
        struct((2 * rows, d), F32),
        [],
        rows * d,
        12 * rows * d,
    )(meta, own, other)


def body(
    tokens, lengths, w_query, b_query, w_key, w_value, b_value, w_out, b_out, gain_one, bias_one,
    w_up, b_up, w_down, b_down, gain_two, bias_two, w_proj, b_proj, cotangent,
):
    n_data = lax.axis_size("dp")
    core = lax.axis_index("tensor")
    d = tokens.shape[1]
    half = w_up.shape[1]
    swap = lambda value: lax.ppermute(value, "tensor", [(0, 1), (1, 0)])
    meta = jnp.array(
        [
            [4, 5, 2, 3, 0, 1, 2, 1, 0, 0, BLK, 1, 1, 1, 0, 0, 0, 1, 2, 0, 0, 1, 2],
            [0, 1, 3, 2, 4, 5, 0, 1, 2, BLK, 0, 0, 0, 0, 1, 1, 1, 1, 2, 0, 0, 1, 2],
        ],
        jnp.int32,
    )[core]

    wup_r, wdn_r, bup_r = swap(w_up), swap(w_down), swap(b_up)
    args = (meta, lengths, tokens, w_query, w_key, w_value, b_query, b_value, w_out)
    *saved_a, part_send, keep_a = attend_fwd(0, 2, *args)
    part_recv = swap(part_send)
    *saved_b, keep_b = attend_fwd(2, 1, *args)
    vecs = jnp.stack([b_out, gain_one, bias_one, b_down, gain_two, bias_two, b_out, b_out])
    (active, slope, hlow, xhat_one, rstd_one, dlow, emb, gproj, sums_two, sums_proj) = ffn_fwd(
        meta, tokens, keep_a, keep_b, part_recv, cotangent, w_up, wup_r, w_down, wdn_r, b_up, bup_r, w_proj, vecs, b_proj
    )
    emb_r = swap(emb)

    if n_data == 16:
        bits_a, bits_b = (1, 4, 2, 8), (2, 4, 1, 8)
    else:
        bits_a = tuple(1 << b for b in range(n_data.bit_length() - 1))
        bits_b = bits_a
    shards = 16
    ids = jnp.stack([place_id(bits_a), place_id(bits_b)]).astype(jnp.int32)
    if n_data != shards:
        ids = jnp.zeros((2,), jnp.int32)

    def chain(keep_a, send_a, keep_b, send_b):
        parts = [(keep_a, send_a), (keep_b, send_b)]
        return Chain(parts, (bits_a, bits_b), n_data) if n_data == shards else Plain(parts)

    other = down_other(active, dlow)
    other_r, gproj_r = swap(other), swap(gproj)
    pre, sums_up = grad_pre(*after((dlow, w_down, wdn_r, slope), other))
    other_r = after(other_r, sums_up)
    ch_d = chain(*down_own(shards, ids, active, dlow, other_r, gproj, gproj_r))

    other = up_other(*after((hlow, pre), ch_d.token))
    other_r = swap(other)
    mix, sums_one = grad_hone(*after((pre, w_up, wup_r, dlow, xhat_one, rstd_one, gain_one), other))
    mix_r = swap(mix)
    ch_u = chain(*up_own(shards, ids, *after((hlow, pre, other_r), sums_one)))
    token = ch_d.advance(ch_u.token)

    weights = (w_query, w_key, w_value, w_out)
    bwd = []
    for s in range(3):
        ins = after((saved_a if s < 2 else saved_b, mix, mix_r), token, ch_u.token)
        bwd.append(attend_bwd(s, meta, lengths, *ins, *weights))
        token = bwd[-1][2]
        if s == 1:
            token = ch_d.advance(token)
            token = ch_u.advance(token)
        if s == 2:
            token = ch_d.advance(token)
    away = jnp.concatenate([bwd[1][1][BLK:], bwd[0][1]], axis=0)
    home = jnp.concatenate([bwd[1][1][:BLK], bwd[2][1]], axis=0)
    away_r = swap(away)
    ins = after((tokens, [b[0] for b in bwd], saved_a[3], saved_b[3], mix, mix_r), token)
    ch_a = chain(*attn_weights(shards, meta, ids, *ins))
    token = ch_a.token

    up_sums = jnp.sum(sums_up, axis=0)
    qv = bwd[0][2] + bwd[1][2] + bwd[2][2]
    mine_up = jnp.concatenate(
        [
            jnp.where(core == 0, up_sums[:half], up_sums[half:]),
            jnp.where(core == 0, up_sums[half:], up_sums[:half]),
        ]
    )
    width = w_query.shape[1]
    by_core_qv = jnp.where(
        (jnp.arange(2) == core)[:, None, None], qv[None, 0:2, :], jnp.zeros((2, 2, width), F32)
    )
    flat = jnp.concatenate(
        [
            sums_two[0:3].reshape(-1), sums_one[0:3].reshape(-1), jnp.sum(sums_proj, axis=0),
            mine_up, by_core_qv.reshape(-1),
        ]
    )
    size = flat.shape[0]
    flat = jnp.pad(flat, (0, -size % 1024)).reshape(8, -1)
    steps = [swap] + [functools.partial(exchange, bit=1 << b, n_data=n_data) for b in range(n_data.bit_length() - 1)]

    def vector_hop(value, token):
        value = after(value, token)
        return value + steps.pop(0)(value)

    home, away_r = after((home, away_r), token)
    grad_rows = (mix.astype(F32) + home.astype(F32) + away_r.astype(F32)).astype(BF16)
    grad_rows_r = swap(grad_rows)
    flat = vector_hop(flat, grad_rows)
    order = ["d", "u", "v", "d", "u", "a", "v", "d", "u", "v", "a", "d", "u", "v", "a", "u", "a", "u", "a", "a", "a", "a"]
    token = flat
    for name in order:
        if name == "v":
            if steps:
                flat = token = vector_hop(flat, token)
        else:
            token = {"d": ch_d, "u": ch_u, "a": ch_a}[name].advance(token)
    while steps:
        flat = vector_hop(flat, token)
    flat = flat.reshape(-1)[:size]
    grad_tokens = finish_tokens(meta, grad_rows, grad_rows_r)

    emb_pick = lambda a, b: jnp.where(core == 0, a, b)
    first = emb_pick(jnp.concatenate([emb[BLK:], emb[:BLK]]), jnp.concatenate([emb_r[BLK:], emb_r[:BLK]]))
    embeddings = jnp.concatenate([first, emb_pick(emb_r, emb)])

    vec = lambda i: flat[i * d:(i + 1) * d]
    at = 6 * d + 128
    g_bproj = flat[6 * d:at]
    g_bup = lax.dynamic_slice(flat, (at + core * half,), (half,))
    qv_all = flat[at + 2 * half:].reshape(2, 2, width)
    g_qv = jnp.where(core == 0, qv_all[0], qv_all[1])

    g_down, g_proj = unpack_down(shards, ids, ch_d.result())
    g_up = unpack_up(shards, ids, ch_u.result())
    g_query, g_key, g_value, g_out = unpack_attn(shards, ids, ch_a.result())
    return (
        embeddings, grad_tokens, g_query, g_qv[0], g_key, g_value, g_qv[1], g_out,
        vec(3), vec(4), vec(5), g_up, g_bup, g_down, vec(0), vec(1), vec(2), g_proj.T, g_bproj,
    )


def solution(mesh):
    rows, cols, split = P("dp", None), P(None, "tensor"), P("tensor")
    return jax.shard_map(
        body,
        mesh=mesh,
        in_specs=(
            rows, P("dp"), cols, split, cols, cols, split, P("tensor", None), P(), P(), P(),
            cols, split, P("tensor", None), P(), P(), P(), P(), P(), rows,
        ),
        out_specs=(
            rows, rows, cols, split, cols, cols, split, P("tensor", None), P(), P(), P(),
            cols, split, P("tensor", None), P(), P(), P(), P(), P(),
        ),
        check_vma=False,
    )
```

```python
import functools

import jax
import jax.numpy as jnp
from jax import lax
from jax.experimental import pallas as pl
from jax.experimental.pallas import tpu as pltpu
from jax.sharding import PartitionSpec as P

HEAD = 64
EPS_NORM = 1e-12
EPS_UNIT = 1e-06
MASKED = -1000000000.0
F32 = jnp.float32
BF16 = jnp.bfloat16
BLK = 256
ANY = pl.ANY
SMALL = ('grad_up_own', 'attend_bwd', 'attn_weights')
TAIL = (
    "rows", "d", "u", "d", "a", "emb", "u", "d", "tokens", "u", "a", "u", "d", "a", "u", "a", "down", "a", "up", "a", "a",
)


def nn(a, b):
    return lax.dot_general(a, b, (((1,), (0,)), ((), ())), preferred_element_type=F32)


def nt(a, b):
    return lax.dot_general(a, b, (((1,), (1,)), ((), ())), preferred_element_type=F32)


def tn(a, b):
    return lax.dot_general(a, b, (((0,), (0,)), ((), ())), preferred_element_type=F32)


def whole(shape):
    zeros = (0,) * len(shape)
    return pl.BlockSpec(shape, lambda *_: zeros, pipeline_mode=pl.Buffered(1))


def out_whole(shape):
    zeros = (0,) * len(shape)
    return pl.BlockSpec(shape, lambda *_: zeros)


def struct(shape, dtype):
    return jax.ShapeDtypeStruct(shape, dtype)


def call(kernel, name, grid, scalars, in_specs, out_specs, out_shape, scratch, flops, nbytes):
    return pl.pallas_call(
        kernel,
        name=name,
        grid_spec=pltpu.PrefetchScalarGridSpec(
            num_scalar_prefetch=scalars,
            grid=grid,
            in_specs=in_specs,
            out_specs=out_specs,
            scratch_shapes=scratch,
        ),
        out_shape=out_shape,
        cost_estimate=pl.CostEstimate(flops=flops, bytes_accessed=nbytes, transcendentals=0),
        compiler_params=pltpu.CompilerParams(vmem_limit_bytes=(24 if name.startswith(SMALL) else 60) * 1024 * 1024),
    )


def pair_lanes(head):
    lane = lax.broadcasted_iota(jnp.int32, (1, 128), 1)
    return (lane < HEAD) if head == 0 else (lane >= HEAD)


def attend_fwd_kernel(n_pairs, first, meta, lens, x0, x1, wq, wk, wv, bq, bv, wo, *rest):
    q_out, k_out, v_out, c_out, lse_out = rest[:5]
    wcat = rest[-1]
    width = n_pairs * 128
    step = pl.program_id(0)
    passage = step + first

    @pl.when(step == 0)
    def _():
        wcat[:, 0:width] = wq[...]
        wcat[:, width:2 * width] = wk[...]
        wcat[:, 2 * width:3 * width] = wv[...]

    for part, x in ((0, x0), (1, x1)):
        rows = slice(part * BLK, (part + 1) * BLK)
        acc = nn(x[...], wcat[...])
        q_out[rows, :] = ((acc[:, 0:width] + bq[...]).astype(BF16) * jnp.bfloat16(0.125)).astype(BF16)
        k_out[rows, :] = acc[:, width:2 * width].astype(BF16)
        v_out[rows, :] = (acc[:, 2 * width:3 * width] + bv[...]).astype(BF16)
    length = lens[meta[6 + passage]]
    place = lax.broadcasted_iota(jnp.int32, (1, 2 * BLK), 1)
    middle = passage == 1
    place = jnp.where(
        place < BLK,
        place + jnp.where(middle, meta[9], 0),
        place + jnp.where(middle, meta[10] - BLK, 0),
    )
    bias = jnp.where(place < length, 0.0, MASKED)

    head_lane = lax.broadcasted_iota(jnp.int32, (1, 128), 1)
    stats = jnp.zeros((2 * BLK, 128), F32)
    for pair in range(n_pairs):
        cols = slice(pair * 128, (pair + 1) * 128)
        qp, kp, vp = q_out[:, cols], k_out[:, cols], v_out[:, cols]
        mixed = None
        for head in range(2):
            lanes = pair_lanes(head)
            scores = nt(jnp.where(lanes, qp, jnp.zeros_like(qp)), kp) + bias
            top = jnp.max(scores, axis=-1, keepdims=True)
            shifted = jnp.exp(scores - top)
            total = jnp.sum(shifted, axis=-1, keepdims=True)
            part = nn(shifted.astype(BF16), vp) * (1.0 / total)
            mixed = part if head == 0 else jnp.where(lanes, part, mixed)
            stats = jnp.where(head_lane == 2 * pair + head, top + jnp.log(total), stats)
        c_out[:, cols] = mixed.astype(BF16)
    lse_out[0] = jnp.transpose(stats)[0:8, :]
    if first == 0:
        send, keep = rest[5:7]

        @pl.when(step == 0)
        def _():
            send[BLK:3 * BLK, :] = nn(c_out[...], wo[...]).astype(BF16)

        @pl.when(step == 1)
        def _():
            keep[...] = nn(c_out[0:BLK, :], wo[...]).astype(BF16)
            send[0:BLK, :] = nn(c_out[BLK:2 * BLK, :], wo[...]).astype(BF16)
    else:
        rest[5][...] = nn(c_out[...], wo[...]).astype(BF16)


def attend_fwd(first, steps, meta, lens, tokens, wq, wk, wv, bq, bv, wo):
    d, width = wq.shape
    n_pairs = width // 128
    seq = 2 * BLK
    rows = steps * seq

    def x_map(part):
        return lambda i, meta, lens: (meta[2 * (i + first) + part], 0)

    blk = pl.BlockSpec((seq, width), lambda i, *_: (i, 0))
    outs = [struct((rows, width), BF16)] * 4 + [struct((steps, 8, seq), F32)]
    specs = [blk] * 4 + [pl.BlockSpec((1, 8, seq), lambda i, *_: (i, 0, 0))]
    if first == 0:
        outs += [struct((3 * BLK, d), BF16), struct((BLK, d), BF16)]
        specs += [out_whole((3 * BLK, d)), out_whole((BLK, d))]
    else:
        outs += [struct((seq, d), BF16)]
        specs += [out_whole((seq, d))]
    return call(
        functools.partial(attend_fwd_kernel, n_pairs, first),
        f"attend_fwd_{first}",
        (steps,),
        2,
        [
            pl.BlockSpec((BLK, d), x_map(0)),
            pl.BlockSpec((BLK, d), x_map(1)),
            whole(wq.shape), whole(wk.shape), whole(wv.shape),
            whole((1, width)), whole((1, width)), whole(wo.shape),
        ],
        specs,
        outs,
        [pltpu.VMEM((d, 3 * width), BF16)],
        8 * rows * d * width + 8 * rows * seq * width,
        4 * rows * d + 8 * d * width + 10 * rows * width,
    )(meta, lens, tokens, tokens, wq, wk, wv, bq.reshape(1, -1), bv.reshape(1, -1), wo)


def phi_pair(u):
    size = jnp.abs(u)
    t = 1.0 / (1.0 + (0.3275911 * 0.7071067811865476) * size)
    e = jnp.exp(u * u * (-0.5))
    poly = t * (0.127414796 + t * (-0.142248368 + t * (0.7107068705 + t * (-0.7265760135 + t * 0.5307027145))))
    tail = poly * e
    phi = jnp.where(u >= 0, 1.0 - tail, tail)
    return u * phi, phi + u * (e * 0.3989422804014327)


def feed_forward_kernel(
    meta, tok, keep_a, keep_b, recv, cot, wup_o, wup_r, wdn_o, wdn_r, bup_o, bup_r, wproj, vecs, bproj,
    active, pre_out, hlow, dlow, mix, emb_out, gproj, sums, psum, usum,
    wup, wdn, slope, h_one, xhat_one, rstd_one, acc, pre, rstd_two, gtwo, hfin, acc8, gp_acc, sems,
):
    step = pl.program_id(0)
    d = tok.shape[1]
    half = wup_o.shape[1]
    copies = (
        pltpu.make_async_copy(wup_o, wup.at[0], sems.at[0]),
        pltpu.make_async_copy(wup_r, wup.at[1], sems.at[1]),
        pltpu.make_async_copy(wdn_o, wdn.at[0], sems.at[2]),
        pltpu.make_async_copy(wdn_r, wdn.at[1], sems.at[3]),
    )

    @pl.when(step == 0)
    def _():
        for item in (0, 2, 1, 3):
            copies[item].start()
        acc8[...] = jnp.zeros_like(acc8)
        gp_acc[...] = jnp.zeros_like(gp_acc)
        psum[...] = jnp.zeros_like(psum)
        usum[...] = jnp.zeros_like(usum)

    chunk = 32
    first = step == 0

    @pl.loop(0, BLK // chunk, unroll=8)
    def _(it):
        rows = pl.ds(pl.multiple_of(it * chunk, chunk), chunk)
        mine = jnp.where(first, keep_a[rows, :].astype(F32), keep_b[rows, :].astype(F32))
        r = tok[rows, :].astype(F32) + (mine + recv[rows, :].astype(F32)) + vecs[0:1, :]
        center = r - jnp.mean(r, axis=-1, keepdims=True)
        rstd = lax.rsqrt(jnp.mean(center * center, axis=-1, keepdims=True) + EPS_NORM)
        xhat = center * rstd
        h = xhat * vecs[1:2, :] + vecs[2:3, :]
        h_one[rows, :] = h
        hlow[rows, :] = h.astype(BF16)
        xhat_one[rows, :] = xhat
        rstd_one[rows, :] = jnp.broadcast_to(rstd, (chunk, 128))

    tile = 512
    per = half // tile
    n_tiles = 2 * per

    def up(j, slot):
        who, col = j // per, (j % per) * tile
        if per and j % per == 0:
            @pl.when(first)
            def _():
                copies[who].wait()
        pre[slot] = nn(hlow[...], wup[who, :, col:col + tile])

    def act(j, slot):
        who, col = j // per, (j % per) * tile
        bias = (bup_o, bup_r)[who][:, col:col + tile]
        out = j * tile
        for r in range(0, BLK, 16):
            value, grad = phi_pair(pre[slot, r:r + 16, :] + bias)
            active[r:r + 16, out:out + tile] = value.astype(BF16)
            slope[r:r + 16, out:out + tile] = grad.astype(BF16)

    def down(j):
        who, row = j // per, (j % per) * tile
        if j % per == 0:
            @pl.when(first)
            def _():
                copies[2 + who].wait()
        part = nn(active[:, j * tile:(j + 1) * tile], wdn[who, row:row + tile, :])
        if j == 0:
            acc[...] = part
        else:
            acc[...] += part

    up(0, 0)
    for j in range(n_tiles):
        if j + 1 < n_tiles:
            up(j + 1, (j + 1) % 2)
        act(j, j % 2)
        down(j)

    @pl.loop(0, BLK // chunk, unroll=8)
    def _(it):
        rows = pl.ds(pl.multiple_of(it * chunk, chunk), chunk)
        r = h_one[rows, :] + acc[rows, :] + vecs[3:4, :]
        center = r - jnp.mean(r, axis=-1, keepdims=True)
        rstd = lax.rsqrt(jnp.mean(center * center, axis=-1, keepdims=True) + EPS_NORM)
        xhat = center * rstd
        acc[rows, :] = xhat
        rstd_two[rows, :] = jnp.broadcast_to(rstd, (chunk, 128))
        hfin[rows, :] = (xhat * vecs[4:5, :] + vecs[5:6, :]).astype(BF16)

    emb = nn(hfin[...], wproj[...]) + bproj[...]
    norm = lax.rsqrt(jnp.sum(emb * emb, axis=-1, keepdims=True) + EPS_UNIT)
    unit = emb * norm
    emb_out[...] = unit.astype(BF16)
    c = cot[...].astype(F32)
    ge = norm * (c - unit * jnp.sum(unit * c, axis=-1, keepdims=True))
    psum[...] += jnp.sum(ge.reshape(BLK // 8, 8, 128), axis=0)
    gelow = ge.astype(BF16)
    gp_acc[...] += tn(gelow, hfin[...])
    gtwo[...] = nt(gelow, wproj[...])

    @pl.loop(0, BLK // chunk, unroll=8)
    def _(it):
        rows = pl.ds(pl.multiple_of(it * chunk, chunk), chunk)
        dy = gtwo[rows, :]
        xhat = acc[rows, :]
        dz = dy * vecs[4:5, :]
        m_one = jnp.mean(dz, axis=-1, keepdims=True)
        m_two = jnp.mean(dz * xhat, axis=-1, keepdims=True)
        gr = (dz - m_one - xhat * m_two) * rstd_two[rows, 0:1]
        gtwo[rows, :] = gr
        dlow[rows, :] = gr.astype(BF16)
        acc8[0] += jnp.sum(gr.reshape(chunk // 8, 8, d), axis=0)
        acc8[1] += jnp.sum((dy * xhat).reshape(chunk // 8, 8, d), axis=0)
        acc8[2] += jnp.sum(dy.reshape(chunk // 8, 8, d), axis=0)

    def up_back(j, slot):
        who, row = j // per, (j % per) * tile
        pre[slot] = nt(dlow[...], wdn[who, row:row + tile, :])

    def act_back(j, slot):
        cols = slice(j * tile, (j + 1) * tile)
        total = jnp.zeros((8, tile), F32)
        for r in range(0, BLK, 16):
            grad = pre[slot, r:r + 16, :] * slope[r:r + 16, cols].astype(F32)
            pre_out[r:r + 16, cols] = grad.astype(BF16)
            total = total + (grad[0:8] + grad[8:16])
        usum[:, cols] += total

    def down_back(j):
        who, col = j // per, (j % per) * tile
        part = nt(pre_out[:, j * tile:(j + 1) * tile], wup[who, :, col:col + tile])
        if j == 0:
            acc[...] = part
        else:
            acc[...] += part

    up_back(0, 0)
    for j in range(n_tiles):
        if j + 1 < n_tiles:
            up_back(j + 1, (j + 1) % 2)
        act_back(j, j % 2)
        down_back(j)

    @pl.loop(0, BLK // chunk, unroll=8)
    def _(it):
        rows = pl.ds(pl.multiple_of(it * chunk, chunk), chunk)
        dy = acc[rows, :] + gtwo[rows, :]
        xhat = xhat_one[rows, :]
        dz = dy * vecs[1:2, :]
        m_one = jnp.mean(dz, axis=-1, keepdims=True)
        m_two = jnp.mean(dz * xhat, axis=-1, keepdims=True)
        gr = (dz - m_one - xhat * m_two) * rstd_one[rows, 0:1]
        mix[rows, :] = gr.astype(BF16)
        acc8[3] += jnp.sum(gr.reshape(chunk // 8, 8, d), axis=0)
        acc8[4] += jnp.sum((dy * xhat).reshape(chunk // 8, 8, d), axis=0)
        acc8[5] += jnp.sum(dy.reshape(chunk // 8, 8, d), axis=0)

    @pl.when(step == pl.num_programs(0) - 1)
    def _():
        gproj[...] = gp_acc[...].astype(BF16)
        for row in range(6):
            sums[row:row + 1, :] = jnp.sum(acc8[row], axis=0, keepdims=True)
        sums[6:8, :] = jnp.zeros((2, d), F32)


def feed_forward(meta, tokens, keep_a, keep_b, recv, cot, wup_o, wup_r, wdn_o, wdn_r, bup_o, bup_r, wproj, vecs, bproj):
    d, half = wup_o.shape
    rows = 3 * BLK
    proj = wproj.shape[1]
    row_map = lambda i, meta: (i, 0)
    tok_map = lambda i, meta: (meta[jnp.where(i == 0, 2, 3 + i)], 0)
    any_spec = pl.BlockSpec(memory_space=ANY)
    return call(
        feed_forward_kernel,
        "feed_forward",
        (3,),
        1,
        [
            pl.BlockSpec((BLK, d), tok_map),
            whole((BLK, d)),
            pl.BlockSpec((BLK, d), lambda i, meta: (jnp.maximum(i - 1, 0), 0)),
            pl.BlockSpec((BLK, d), row_map),
            pl.BlockSpec((BLK, proj), tok_map),
            any_spec, any_spec, any_spec, any_spec,
            whole((1, half)), whole((1, half)),
            whole(wproj.shape), whole((8, d)), whole((1, proj)),
        ],
        [
            pl.BlockSpec((BLK, 2 * half), row_map),
            pl.BlockSpec((BLK, 2 * half), row_map),
            pl.BlockSpec((BLK, d), row_map),
            pl.BlockSpec((BLK, d), row_map),
            pl.BlockSpec((BLK, d), row_map),
            pl.BlockSpec((BLK, proj), row_map),
            out_whole((proj, d)),
            out_whole((8, d)),
            out_whole((8, proj)),
            out_whole((8, 2 * half)),
        ],
        [
            struct((rows, 2 * half), BF16),
            struct((rows, 2 * half), BF16),
            struct((rows, d), BF16),
            struct((rows, d), BF16),
            struct((rows, d), BF16),
            struct((rows, proj), BF16),
            struct((proj, d), BF16),
            struct((8, d), F32),
            struct((8, proj), F32),
            struct((8, 2 * half), F32),
        ],
        [
            pltpu.VMEM((2, d, half), BF16),
            pltpu.VMEM((2, half, d), BF16),
            pltpu.VMEM((BLK, 2 * half), BF16),
            pltpu.VMEM((BLK, d), F32),
            pltpu.VMEM((BLK, d), F32),
            pltpu.VMEM((BLK, 128), F32),
            pltpu.VMEM((BLK, d), F32),
            pltpu.VMEM((2, BLK, 512), F32),
            pltpu.VMEM((BLK, 128), F32),
            pltpu.VMEM((BLK, d), F32),
            pltpu.VMEM((BLK, d), BF16),
            pltpu.VMEM((6, 8, d), F32),
            pltpu.VMEM((proj, d), F32),
            pltpu.SemaphoreType.DMA((4,)),
        ],
        16 * rows * d * half + 6 * rows * d * proj,
        8 * d * half + 8 * rows * half + 12 * rows * d,
    )(
        meta, tokens, keep_a, keep_b, recv, cot, wup_o, wup_r, wdn_o, wdn_r,
        bup_o.reshape(1, -1), bup_r.reshape(1, -1), wproj, vecs, bproj.reshape(1, -1),
    )


def down_other_kernel(act, dlow, out):
    out[...] = tn(act[...], dlow[...]).astype(BF16)


def down_other(active, dlow):
    rows, d = dlow.shape
    half = active.shape[1] // 2
    tile = 256
    shift = half // tile
    return call(
        down_other_kernel,
        "grad_down_other",
        (half // tile,),
        0,
        [pl.BlockSpec((rows, tile), lambda i: (0, shift + i)), whole((rows, d))],
        pl.BlockSpec((tile, d), lambda i: (i, 0)),
        struct((half, d), BF16),
        [],
        2 * rows * d * half,
        2 * rows * half + 2 * rows * d + 2 * half * d,
    )(active, dlow)


def spread(source, me, shards, rows, outs, at=0):
    middle = shards // 2
    for place in range(shards):
        start = pl.multiple_of(jnp.bitwise_xor(place, me) * rows, 8)
        target = outs[place // middle]
        target[place % middle, at:at + rows, :] = source[pl.ds(start, rows), :].astype(BF16)


def down_own_kernel(shards, ids, act, dlow, recv, gproj, grecv, keep_a, send_a, keep_b, send_b, full, extra):
    step = pl.program_id(0)
    tile = act.shape[1]
    rows = pl.ds(pl.multiple_of(step * tile, tile), tile)
    full[rows, :] = (tn(act[...], dlow[...]) + recv[...].astype(F32)).astype(BF16)

    @pl.when(step == pl.num_programs(0) - 1)
    def _():
        part = full.shape[0] // 2
        per = part // shards
        spread(full.at[0:part], ids[0], shards, per, (keep_a, send_a))
        extra[...] = gproj[...].astype(F32) + grecv[...].astype(F32)
        spread(extra, ids[0], shards, extra.shape[0] // shards, (keep_a, send_a), at=per)
        spread(full.at[part:2 * part], ids[1], shards, per, (keep_b, send_b))


def down_own(shards, ids, active, dlow, recv, gproj, grecv):
    rows, d = dlow.shape
    half = active.shape[1] // 2
    tile = 256
    per = half // 2 // shards
    extra = gproj.shape[0] // shards
    shape_a, shape_b = (shards // 2, per + extra, d), (shards // 2, per, d)
    return call(
        functools.partial(down_own_kernel, shards),
        "grad_down_own",
        (half // tile,),
        1,
        [
            pl.BlockSpec((rows, tile), lambda i, ids: (0, i)),
            whole((rows, d)),
            pl.BlockSpec((tile, d), lambda i, ids: (i, 0)),
            whole(gproj.shape),
            whole(gproj.shape),
        ],
        [out_whole(shape_a)] * 2 + [out_whole(shape_b)] * 2,
        [struct(shape_a, BF16)] * 2 + [struct(shape_b, BF16)] * 2,
        [pltpu.VMEM((half, d), BF16), pltpu.VMEM(gproj.shape, F32)],
        2 * rows * d * half,
        2 * rows * half + 2 * rows * d + 4 * half * d,
    )(ids, active, dlow, recv, gproj, grecv)


def up_other_kernel(hlow, pre, out, flipped):
    @pl.when(pl.program_id(0) == 0)
    def _():
        flipped[...] = jnp.transpose(hlow[...])

    out[...] = nn(flipped[...], pre[...]).astype(BF16)


def up_other(hlow, pre):
    rows, d = hlow.shape
    half = pre.shape[1] // 2
    tile = 512
    shift = half // tile
    return call(
        up_other_kernel,
        "grad_up_other",
        (half // tile,),
        0,
        [whole((rows, d)), pl.BlockSpec((rows, tile), lambda i: (0, shift + i))],
        pl.BlockSpec((d, tile), lambda i: (0, i)),
        struct((d, half), BF16),
        [pltpu.VMEM((d, rows), BF16)],
        2 * rows * d * half,
        2 * rows * half + 2 * rows * d + 2 * half * d,
    )(hlow, pre)


def up_own_kernel(shards, ids, hlow, pre, recv, keep_a, send_a, keep_b, send_b, flipped, full):
    step = pl.program_id(0)
    d = hlow.shape[1]
    tile = pre.shape[1]
    per = d // shards

    @pl.when(step == 0)
    def _():
        flipped[...] = jnp.transpose(hlow[...])

    out = (nn(flipped[...], pre[...]) + recv[...].astype(F32)).astype(BF16)
    full[...] = out
    steps = pl.num_programs(0) // 2
    for part, outs in ((0, (keep_a, send_a)), (1, (keep_b, send_b))):
        for place in range(2):
            @pl.when(step == part * 2 + place)
            def _(part=part, outs=outs, place=place):
                for j in range(shards):
                    start = pl.multiple_of(jnp.bitwise_xor(j, ids[part]) * per, 8)
                    outs[j // (shards // 2)][j % (shards // 2), :, place * tile:(place + 1) * tile] = full[
                        pl.ds(start, per), :
                    ]


def up_own(shards, ids, hlow, pre, recv):
    rows, d = hlow.shape
    half = pre.shape[1] // 2
    tile = half // 4
    shape = (shards // 2, d // shards, half // 2)
    return call(
        functools.partial(up_own_kernel, shards),
        "grad_up_own",
        (4,),
        1,
        [
            whole((rows, d)),
            pl.BlockSpec((rows, tile), lambda i, ids: (0, i)),
            pl.BlockSpec((d, tile), lambda i, ids: (0, i)),
        ],
        [out_whole(shape)] * 4,
        [struct(shape, BF16)] * 4,
        [pltpu.VMEM((d, rows), BF16), pltpu.VMEM((d, tile), BF16)],
        2 * rows * d * half,
        2 * rows * half + 2 * rows * d + 4 * half * d,
    )(ids, hlow, pre, recv)


def attend_bwd_kernel(n_pairs, passage, meta, lens, q, k, v, ctx, lse, mix0, mix1, wq, wk, wv, wo, *rest):
    dqkv, dx, sums, gctx, wcat, deltas, lser = rest
    width = n_pairs * 128
    seq = 2 * BLK
    wcat[:, 0:width] = wq[...]
    wcat[:, width:2 * width] = wk[...]
    wcat[:, 2 * width:3 * width] = wv[...]
    for part, mix in ((0, mix0), (1, mix1)):
        gctx[part * BLK:(part + 1) * BLK, :] = nt(mix[...], wo[...]).astype(BF16)
    length = lens[meta[6 + passage]]
    place = lax.broadcasted_iota(jnp.int32, (seq, 1), 0)
    if passage == 1:
        place = jnp.where(place < BLK, place + meta[9], place + meta[10] - BLK)
    bias = jnp.where(place < length, 0.0, MASKED)
    both = gctx[...].astype(F32) * ctx[...].astype(F32)
    high = both.astype(BF16)
    low = (both - high.astype(F32)).astype(BF16)
    owner = lax.broadcasted_iota(jnp.int32, (16, width), 1) // HEAD
    member = (owner == lax.broadcasted_iota(jnp.int32, (16, width), 0)).astype(F32).astype(BF16)
    deltas[...] = (nt(member, high) + nt(member, low))[0:8, :]
    lser[...] = lse[0]
    for pair in range(n_pairs):
        cols = slice(pair * 128, (pair + 1) * 128)
        qp, kp, vp, gp = q[:, cols], k[:, cols], v[:, cols], gctx[:, cols]
        kflip = jnp.transpose(kp)
        dk = dv = dq = None
        for head in range(2):
            lanes = pair_lanes(head)
            here = 2 * pair + head
            qm = jnp.where(lanes, qp, jnp.zeros_like(qp))
            gm = jnp.where(lanes, gp, jnp.zeros_like(gp))
            probs = jnp.exp(nt(kp, qm) + bias - lser[here:here + 1, :])
            dprobs = nt(vp, gm)
            dscores = (probs * (dprobs - deltas[here:here + 1, :])).astype(BF16)
            dv_part = nn(probs.astype(BF16), gm)
            dk_part = nn(dscores, qm)
            dq_part = nn(kflip, dscores)
            if head == 0:
                dk, dv, dq = dk_part, dv_part, dq_part
            else:
                row = lax.broadcasted_iota(jnp.int32, (128, 1), 0)
                dk, dv, dq = dk + dk_part, dv + dv_part, jnp.where(row < HEAD, dq, dq_part)
        dq = jnp.transpose(dq) * 0.125
        sums[0:1, cols] = jnp.sum(dq, axis=0, keepdims=True)
        sums[1:2, cols] = jnp.sum(dv, axis=0, keepdims=True)
        dqkv[:, cols] = dq.astype(BF16)
        dqkv[:, width + pair * 128:width + (pair + 1) * 128] = dk.astype(BF16)
        dqkv[:, 2 * width + pair * 128:2 * width + (pair + 1) * 128] = dv.astype(BF16)
    sums[2:8, :] = jnp.zeros((6, width), F32)
    for part in range(2):
        rows = slice(part * BLK, (part + 1) * BLK)
        dx[rows, :] = nt(dqkv[rows, :], wcat[...]).astype(BF16)


def attend_bwd(passage, meta, lens, saved, own, recv, wq, wk, wv, wo):
    d, width = wq.shape
    n_pairs = width // 128
    seq = 2 * BLK
    q, k, v, ctx, lse = saved
    at = passage if passage < 2 else 0
    blk = pl.BlockSpec((seq, width), lambda i, *_: (at, 0))
    first, second = [((recv, 1), (recv, 2)), ((own, 0), (recv, 0)), ((own, 1), (own, 2))][passage]

    def mix_spec(index):
        return pl.BlockSpec((BLK, d), lambda i, *_: (index, 0))

    return call(
        functools.partial(attend_bwd_kernel, n_pairs, passage),
        f"attend_bwd_{passage}",
        (1,),
        2,
        [
            blk, blk, blk, blk,
            pl.BlockSpec((1, 8, seq), lambda i, *_: (at, 0, 0)),
            mix_spec(first[1]), mix_spec(second[1]),
            whole(wq.shape), whole(wk.shape), whole(wv.shape), whole(wo.shape),
        ],
        [out_whole((seq, 3 * width)), out_whole((seq, d)), out_whole((8, width))],
        [struct((seq, 3 * width), BF16), struct((seq, d), BF16), struct((8, width), F32)],
        [
            pltpu.VMEM((seq, width), BF16),
            pltpu.VMEM((d, 3 * width), BF16),
            pltpu.VMEM((8, seq), F32),
            pltpu.VMEM((8, seq), F32),
        ],
        8 * seq * d * width + 20 * seq * seq * width,
        8 * d * width + 16 * seq * width + 4 * seq * d,
    )(meta, lens, q, k, v, ctx, lse, first[0], second[0], wq, wk, wv, wo)


def attn_weights_kernel(
    shards, meta, ids, x0, x1, g0, g1, g2, c0, c1, m0, m1, vec, keep_a, send_a, keep_b, send_b, acc, acc_o, full
):
    step = pl.program_id(0)
    width = c0.shape[1]
    d = x0.shape[1]

    def add(x, grads, ctx, mix, rows, first):
        part = tn(x[...], grads[rows, :])
        part_o = tn(ctx[rows, :], mix)
        if first:
            acc[...] = part
            acc_o[...] = part_o
        else:
            acc[...] += part
            acc_o[...] += part_o

    lo, hi = slice(0, BLK), slice(BLK, 2 * BLK)
    blk = lambda ref, i: ref[i * BLK:(i + 1) * BLK, :]
    own, recv = m0, m1

    @pl.when(step == 0)
    def _():
        add(x0, g0, c0, blk(recv, 1), lo, True)
        add(x1, g0, c0, blk(recv, 2), hi, False)

    @pl.when(step == 1)
    def _():
        mid_lo, mid_hi = slice(2 * BLK, 3 * BLK), slice(3 * BLK, 4 * BLK)
        acc[...] += tn(x0[...], g1[lo, :]) + tn(x1[...], g1[hi, :])
        acc_o[...] += tn(c0[mid_lo, :], blk(own, 0)) + tn(c0[mid_hi, :], blk(recv, 0))

    @pl.when(step == 2)
    def _():
        add(x0, g2, c1, blk(own, 1), lo, False)
        add(x1, g2, c1, blk(own, 2), hi, False)
        full[:, 0:2 * width] = acc[:, 0:2 * width].astype(BF16)
        spread(full, ids[0], shards, d // shards, (keep_a, send_a))
        spread(vec, ids[0], shards, vec.shape[0] // shards, (keep_a, send_a), at=d // shards)
        full[:, 0:width] = acc[:, 2 * width:3 * width].astype(BF16)
        full[0:width, width:2 * width] = acc_o[:, 0:width].astype(BF16)
        full[width:2 * width, width:2 * width] = acc_o[:, width:2 * width].astype(BF16)
        spread(full, ids[1], shards, d // shards, (keep_b, send_b))


def attn_weights(shards, meta, ids, tokens, grads, ctx_a, ctx_b, own, recv, vec):
    d = tokens.shape[1]
    width = ctx_a.shape[1]
    seq = 2 * BLK
    shape_b = (shards // 2, d // shards, 2 * width)
    shape_a = (shards // 2, d // shards + vec.shape[0] // shards, 2 * width)
    rows = 3 * seq

    def x_map(part):
        return lambda i, meta, ids: (meta[2 * i + part], 0)

    return call(
        functools.partial(attn_weights_kernel, shards),
        "attn_weights",
        (3,),
        2,
        [
            pl.BlockSpec((BLK, d), x_map(0)),
            pl.BlockSpec((BLK, d), x_map(1)),
            whole((seq, 3 * width)), whole((seq, 3 * width)), whole((seq, 3 * width)),
            whole(ctx_a.shape), whole(ctx_b.shape),
            whole(own.shape), whole(recv.shape), whole(vec.shape),
        ],
        [out_whole(shape_a)] * 2 + [out_whole(shape_b)] * 2,
        [struct(shape_a, BF16)] * 2 + [struct(shape_b, BF16)] * 2,
        [pltpu.VMEM((d, 3 * width), F32), pltpu.VMEM((width, d), F32), pltpu.VMEM((d, 2 * width), BF16)],
        8 * rows * d * width,
        4 * rows * d + 8 * rows * width + 8 * d * width,
    )(meta, ids, tokens, tokens, grads[0], grads[1], grads[2], ctx_a, ctx_b, own, recv, vec)


def after(value, *tokens):
    leaves, tree = jax.tree.flatten(value)
    out = lax.optimization_barrier((*leaves, *tokens))
    return jax.tree.unflatten(tree, out[: len(leaves)])


def exchange(value, bit, n_data):
    return lax.ppermute(value, "dp", [(i, i ^ bit) for i in range(n_data)])


def add_low(a, b):
    return (a.astype(F32) + b.astype(F32)).astype(BF16)


class Chain:
    def __init__(self, parts, orders, n_data):
        self.orders, self.n_data = orders, n_data
        self.hop = 0
        self.keep = [keep for keep, _ in parts]
        self.send([send for _, send in parts])

    def bit(self, part):
        order = self.orders[part]
        return (order + order[::-1])[self.hop]

    def send(self, values):
        self.token = values[-1]
        self.got = [exchange(value, self.bit(i), self.n_data) for i, value in enumerate(values)]
        self.hop += 1

    def advance(self, *tokens):
        self.keep, self.got = after((self.keep, self.got), *tokens)
        hops = len(self.orders[0])
        if self.hop < hops:
            half = [keep.shape[0] // 2 for keep in self.keep]
            sends = [add_low(k[h:], g[h:]) for k, g, h in zip(self.keep, self.got, half)]
            self.keep = [add_low(k[:h], g[:h]) for k, g, h in zip(self.keep, self.got, half)]
            self.send(sends)
        elif self.hop == hops:
            self.keep = [add_low(k, g) for k, g in zip(self.keep, self.got)]
            self.send(self.keep)
        elif self.hop < 2 * hops:
            self.keep = [jnp.concatenate([k, g]) for k, g in zip(self.keep, self.got)]
            self.send(self.keep)
        return self.token

    def result(self):
        return list(zip(self.keep, self.got))


class Plain:
    def __init__(self, parts):
        sums = [lax.psum(jnp.concatenate(part), "dp") for part in parts]
        self.pairs = [(total[: total.shape[0] // 2], total[total.shape[0] // 2:]) for total in sums]
        self.token = sums[-1]

    def advance(self, *tokens):
        return self.token

    def result(self):
        return self.pairs


def place_id(bits):
    me = lax.axis_index("dp")
    value = 0
    for bit in bits:
        value = value * 2 + jnp.where(jnp.bitwise_and(me, bit) != 0, 1, 0)
    return value


def picked(low, high, place, half, rows):
    at = jnp.bitwise_and(place, half - 1)
    return jnp.where(place < half, low[at, rows, :].astype(F32), high[at, rows, :].astype(F32))


def unpack_down_kernel(shards, per, ids, low_a, high_a, low_b, high_b, out, extra):
    step = pl.program_id(0)
    half, group = shards // 2, shards // 4
    more = low_a.shape[1] - per
    for part, (low, high) in enumerate(((low_a, high_a), (low_b, high_b))):
        @pl.when(step // 4 == part)
        def _(part=part, low=low, high=high):
            for q in range(group):
                shard = (step % 4) * group + q
                place = jnp.bitwise_xor(shard, ids[part])
                out[q * per:(q + 1) * per, :] = picked(low, high, place, half, slice(0, per))
                if part == 0:
                    rows = pl.ds(pl.multiple_of(shard * more, more), more)
                    extra[rows, :] = picked(low, high, place, half, slice(per, per + more))


def unpack_down(shards, ids, parts):
    args = [array for part in parts for array in part]
    d = args[0].shape[2]
    per = args[2].shape[1]
    more = args[0].shape[1] - per
    rows = 2 * shards * per
    return call(
        functools.partial(unpack_down_kernel, shards, per),
        "unpack_down",
        (8,),
        1,
        [whole(array.shape) for array in args],
        [pl.BlockSpec((rows // 8, d), lambda i, ids: (i, 0)), out_whole((shards * more, d))],
        [struct((rows, d), F32), struct((shards * more, d), F32)],
        [],
        rows * d,
        6 * rows * d,
    )(ids, *args)


def unpack_up_kernel(shards, ids, low_a, high_a, low_b, high_b, out):
    step = pl.program_id(0)
    half, group = shards // 2, shards // 4
    per, wide = low_a.shape[1:]
    for part, (low, high) in enumerate(((low_a, high_a), (low_b, high_b))):
        for q in range(group):
            place = jnp.bitwise_xor(step * group + q, ids[part])
            out[q * per:(q + 1) * per, part * wide:(part + 1) * wide] = picked(low, high, place, half, slice(None))


def unpack_up(shards, ids, parts):
    args = [array for part in parts for array in part]
    per, wide = args[0].shape[1:]
    rows = shards * per
    return call(
        functools.partial(unpack_up_kernel, shards),
        "unpack_up",
        (4,),
        1,
        [whole(array.shape) for array in args],
        pl.BlockSpec((rows // 4, 2 * wide), lambda i, ids: (i, 0)),
        struct((rows, 2 * wide), F32),
        [],
        2 * rows * wide,
        12 * rows * wide,
    )(ids, *args)


def unpack_attn_kernel(shards, per, ids, low_a, high_a, low_b, high_b, query, key, value, out, vec):
    step = pl.program_id(0)
    half, group = shards // 2, shards // 4
    width = low_b.shape[2] // 2
    more = low_a.shape[1] - per
    every = slice(None)
    for q in range(group):
        shard = step * group + q
        rows = slice(q * per, (q + 1) * per)
        place = jnp.bitwise_xor(shard, ids[0])
        both = picked(low_a, high_a, place, half, slice(0, per))
        query[rows, :], key[rows, :] = both[:, :width], both[:, width:]
        vec[q * more:(q + 1) * more, :] = picked(low_a, high_a, place, half, slice(per, per + more))
        value[rows, :] = picked(low_b, high_b, jnp.bitwise_xor(shard, ids[1]), half, every)[:, :width]
    for q in range(group // 2):
        rows = slice(q * per, (q + 1) * per)
        for side in range(2):
            shard = step * (group // 2) + q + side * half
            both = picked(low_b, high_b, jnp.bitwise_xor(shard, ids[1]), half, every)
            out[rows, side * width:(side + 1) * width] = both[:, width:]


def unpack_attn(shards, ids, parts):
    args = [array for part in parts for array in part]
    per, wide = args[2].shape[1:]
    more = args[0].shape[1] - per
    rows, width = shards * per, wide // 2
    spec = pl.BlockSpec((rows // 4, width), lambda i, ids: (i, 0))
    return call(
        functools.partial(unpack_attn_kernel, shards, per),
        "unpack_attn",
        (4,),
        1,
        [whole(array.shape) for array in args],
        [
            spec, spec, spec,
            pl.BlockSpec((width // 4, rows), lambda i, ids: (i, 0)),
            pl.BlockSpec((shards * more // 4, wide), lambda i, ids: (i, 0)),
        ],
        [struct((rows, width), F32)] * 3 + [struct((width, rows), F32), struct((shards * more, wide), F32)],
        [],
        2 * rows * wide,
        12 * rows * wide,
    )(ids, *args)


def finish_kernel(meta, own, other, out):
    step = pl.program_id(0)
    rows = pl.ds(pl.multiple_of(meta[17 + step] * BLK, BLK), BLK)
    out[...] = jnp.where(meta[11 + step] == 1, own[rows, :].astype(F32), other[rows, :].astype(F32))


def finish_tokens(meta, own, other):
    rows, d = own.shape
    return call(
        finish_kernel,
        "grad_tokens",
        (2 * rows // BLK,),
        1,
        [whole((rows, d)), whole((rows, d))],
        pl.BlockSpec((BLK, d), lambda i, meta: (i, 0)),
        struct((2 * rows, d), F32),
        [],
        rows * d,
        12 * rows * d,
    )(meta, own, other)


def body(
    tokens, lengths, w_query, b_query, w_key, w_value, b_value, w_out, b_out, gain_one, bias_one,
    w_up, b_up, w_down, b_down, gain_two, bias_two, w_proj, b_proj, cotangent,
):
    n_data = lax.axis_size("dp")
    core = lax.axis_index("tensor")
    d = tokens.shape[1]
    half = w_up.shape[1]
    swap = lambda value: lax.ppermute(value, "tensor", [(0, 1), (1, 0)])
    meta = jnp.array(
        [
            [4, 5, 2, 3, 0, 1, 2, 1, 0, 0, BLK, 1, 1, 1, 0, 0, 0, 1, 2, 0, 0, 1, 2],
            [0, 1, 3, 2, 4, 5, 0, 1, 2, BLK, 0, 0, 0, 0, 1, 1, 1, 1, 2, 0, 0, 1, 2],
        ],
        jnp.int32,
    )[core]

    wup_r, wdn_r, bup_r = swap(w_up), swap(w_down), swap(b_up)
    args = (meta, lengths, tokens, w_query, w_key, w_value, b_query, b_value, w_out)
    *saved_a, part_send, keep_a = attend_fwd(0, 2, *args)
    part_recv = swap(part_send)
    *saved_b, keep_b = attend_fwd(2, 1, *args)
    vecs = jnp.stack([b_out, gain_one, bias_one, b_down, gain_two, bias_two, b_out, b_out])
    active, pre, hlow, dlow, mix, emb, gproj, sums, sums_proj, sums_up = feed_forward(
        meta, tokens, keep_a, keep_b, part_recv, cotangent, w_up, wup_r, w_down, wdn_r, b_up, bup_r, w_proj, vecs, b_proj
    )
    mix_r = swap(mix)
    emb_r = swap(emb)

    if n_data == 16:
        bits_a, bits_b = (1, 4, 2, 8), (2, 4, 1, 8)
    else:
        bits_a = tuple(1 << b for b in range(n_data.bit_length() - 1))
        bits_b = bits_a
    shards = 16
    ids = jnp.stack([place_id(bits_a), place_id(bits_b)]).astype(jnp.int32)
    if n_data != shards:
        ids = jnp.zeros((2,), jnp.int32)

    def chain(keep_a, send_a, keep_b, send_b):
        parts = [(keep_a, send_a), (keep_b, send_b)]
        return Chain(parts, (bits_a, bits_b), n_data) if n_data == shards else Plain(parts)

    down = down_other(active, dlow)
    down_r, gproj_r = swap(down), swap(gproj)
    up = up_other(*after((hlow, pre), down))
    up_r = swap(up)
    ch_d = chain(*down_own(shards, ids, *after((active, dlow, down_r, gproj, gproj_r), up)))
    ch_u = chain(*up_own(shards, ids, *after((hlow, pre, up_r), ch_d.token)))
    token = ch_u.token

    up_sums = jnp.sum(sums_up, axis=0)
    shared = jnp.concatenate([sums[0:6].reshape(-1), jnp.sum(sums_proj, axis=0)])
    mine = jnp.concatenate([shared, up_sums[:half]])
    theirs_r = swap(jnp.concatenate([shared, up_sums[half:]]))

    weights = (w_query, w_key, w_value, w_out)
    bwd = []
    for s in range(3):
        ins = after((saved_a if s < 2 else saved_b, mix, mix_r), token)
        bwd.append(attend_bwd(s, meta, lengths, *ins, *weights))
        token = bwd[-1][2]
        token = (ch_u if s == 1 else ch_d).advance(token)
    qv = bwd[0][2] + bwd[1][2] + bwd[2][2]
    flat = jnp.concatenate([mine + theirs_r, qv[0:2].reshape(-1)])
    size = flat.shape[0]
    room = -size % shards
    vec = jnp.pad(flat, (0, room)).reshape(shards, 1, -1)
    vec = jnp.pad(vec, ((0, 0), (0, 7), (0, d - vec.shape[2]))).reshape(8 * shards, d)
    away = jnp.concatenate([bwd[1][1][BLK:], bwd[0][1]], axis=0)
    home = jnp.concatenate([bwd[1][1][:BLK], bwd[2][1]], axis=0)
    away_r = swap(away)
    ins = after((tokens, [b[0] for b in bwd], saved_a[3], saved_b[3], mix, mix_r, vec), token)
    ch_a = chain(*attn_weights(shards, meta, ids, *ins))
    token = ch_u.advance(ch_d.advance(ch_a.token))

    for name in TAIL:
        if name in "dua":
            token = {"d": ch_d, "u": ch_u, "a": ch_a}[name].advance(token)
        elif name == "rows":
            home, away_r = after((home, away_r), token)
            grad_rows = (mix.astype(F32) + home.astype(F32) + away_r.astype(F32)).astype(BF16)
            grad_rows_r = swap(grad_rows)
            token = grad_rows
        elif name == "tokens":
            grad_tokens = finish_tokens(meta, *after((grad_rows, grad_rows_r), token))
            token = grad_tokens
        elif name == "emb":
            emb, emb_r = after((emb, emb_r), token)
            emb_pick = lambda a, b: jnp.where(core == 0, a, b)
            first = emb_pick(jnp.concatenate([emb[BLK:], emb[:BLK]]), jnp.concatenate([emb_r[BLK:], emb_r[:BLK]]))
            embeddings = jnp.concatenate([first, emb_pick(emb_r, emb)])
            token = embeddings
        elif name == "down":
            g_down, g_proj = unpack_down(shards, ids, after(ch_d.result(), token))
            token = g_proj
        elif name == "up":
            token = g_up = unpack_up(shards, ids, after(ch_u.result(), token))
    g_query, g_key, g_value, g_out, vec = unpack_attn(shards, ids, ch_a.result())
    flat = vec.reshape(shards, 8, d)[:, 0, : (size + room) // shards].reshape(-1)

    width = w_query.shape[1]
    part = lambda i: flat[i * d:(i + 1) * d]
    at = 6 * d + w_proj.shape[1]
    g_bup = flat[at:at + half]
    g_bq, g_bv = flat[at + half:at + half + width], flat[at + half + width:at + half + 2 * width]
    return (
        embeddings, grad_tokens, g_query, g_bq, g_key, g_value, g_bv, g_out,
        part(3), part(4), part(5), g_up, g_bup, g_down, part(0), part(1), part(2), g_proj.T, flat[6 * d:at],
    )


def solution(mesh):
    rows, cols, split = P("dp", None), P(None, "tensor"), P("tensor")
    return jax.shard_map(
        body,
        mesh=mesh,
        in_specs=(
            rows, P("dp"), cols, split, cols, cols, split, P("tensor", None), P(), P(), P(),
            cols, split, P("tensor", None), P(), P(), P(), P(), P(), rows,
        ),
        out_specs=(
            rows, rows, cols, split, cols, cols, split, P("tensor", None), P(), P(), P(),
            cols, split, P("tensor", None), P(), P(), P(), P(), P(),
        ),
        check_vma=False,
    )
```

```python
import functools

import jax
import jax.numpy as jnp
from jax import lax
from jax.experimental import pallas as pl
from jax.experimental.pallas import tpu as pltpu
from jax.sharding import PartitionSpec as P

HEAD = 64
EPS_NORM = 1e-12
EPS_UNIT = 1e-06
MASKED = -1000000000.0
F32 = jnp.float32
BF16 = jnp.bfloat16
BLK = 256
ANY = pl.ANY
SMALL = ('grad_up_own', 'attend_bwd', 'attn_weights')
TAIL = (
    "d", "a", "d", "u", "d", "a", "u", "a", "u", "d", "a", "u", "emb", "a", "rows", "a", "u", "down", "a", "tokens",
    "up",
)


def nn(a, b):
    return lax.dot_general(a, b, (((1,), (0,)), ((), ())), preferred_element_type=F32)


def nt(a, b):
    return lax.dot_general(a, b, (((1,), (1,)), ((), ())), preferred_element_type=F32)


def tn(a, b):
    return lax.dot_general(a, b, (((0,), (0,)), ((), ())), preferred_element_type=F32)


def whole(shape):
    zeros = (0,) * len(shape)
    return pl.BlockSpec(shape, lambda *_: zeros, pipeline_mode=pl.Buffered(1))


def out_whole(shape):
    zeros = (0,) * len(shape)
    return pl.BlockSpec(shape, lambda *_: zeros)


def struct(shape, dtype):
    return jax.ShapeDtypeStruct(shape, dtype)


def call(kernel, name, grid, scalars, in_specs, out_specs, out_shape, scratch, flops, nbytes):
    return pl.pallas_call(
        kernel,
        name=name,
        grid_spec=pltpu.PrefetchScalarGridSpec(
            num_scalar_prefetch=scalars,
            grid=grid,
            in_specs=in_specs,
            out_specs=out_specs,
            scratch_shapes=scratch,
        ),
        out_shape=out_shape,
        cost_estimate=pl.CostEstimate(flops=flops, bytes_accessed=nbytes, transcendentals=0),
        compiler_params=pltpu.CompilerParams(vmem_limit_bytes=(24 if name.startswith(SMALL) else 60) * 1024 * 1024),
    )


def pair_lanes(head):
    lane = lax.broadcasted_iota(jnp.int32, (1, 128), 1)
    return (lane < HEAD) if head == 0 else (lane >= HEAD)


def attend_fwd_kernel(n_pairs, first, meta, lens, x0, x1, wq, wk, wv, bqv, wo, *rest):
    q_out, k_out, v_out, c_out, lse_out = rest[:5]
    wcat = rest[-1]
    width = n_pairs * 128
    step = pl.program_id(0)
    passage = step + first

    @pl.when(step == 0)
    def _():
        wcat[:, 0:width] = wq[...]
        wcat[:, width:2 * width] = wk[...]
        wcat[:, 2 * width:3 * width] = wv[...]

    for part, x in ((0, x0), (1, x1)):
        rows = slice(part * BLK, (part + 1) * BLK)
        acc = nn(x[...], wcat[...])
        q_out[rows, :] = ((acc[:, 0:width] + bqv[0:1, :]).astype(BF16) * jnp.bfloat16(0.125)).astype(BF16)
        k_out[rows, :] = acc[:, width:2 * width].astype(BF16)
        v_out[rows, :] = (acc[:, 2 * width:3 * width] + bqv[1:2, :]).astype(BF16)
    length = lens[meta[6 + passage]]
    place = lax.broadcasted_iota(jnp.int32, (1, 2 * BLK), 1)
    middle = passage == 1
    place = jnp.where(
        place < BLK,
        place + jnp.where(middle, meta[9], 0),
        place + jnp.where(middle, meta[10] - BLK, 0),
    )
    bias = jnp.where(place < length, 0.0, MASKED)

    head_lane = lax.broadcasted_iota(jnp.int32, (1, 128), 1)
    stats = jnp.zeros((2 * BLK, 128), F32)
    for pair in range(n_pairs):
        cols = slice(pair * 128, (pair + 1) * 128)
        qp, kp, vp = q_out[:, cols], k_out[:, cols], v_out[:, cols]
        mixed = None
        for head in range(2):
            lanes = pair_lanes(head)
            scores = nt(jnp.where(lanes, qp, jnp.zeros_like(qp)), kp) + bias
            top = jnp.max(scores, axis=-1, keepdims=True)
            shifted = jnp.exp(scores - top)
            total = jnp.sum(shifted, axis=-1, keepdims=True)
            part = nn(shifted.astype(BF16), vp) * (1.0 / total)
            mixed = part if head == 0 else jnp.where(lanes, part, mixed)
            stats = jnp.where(head_lane == 2 * pair + head, top + jnp.log(total), stats)
        c_out[:, cols] = mixed.astype(BF16)
    lse_out[0] = jnp.transpose(stats)[0:8, :]
    if first == 0:
        send, keep = rest[5:7]

        @pl.when(step == 0)
        def _():
            send[BLK:3 * BLK, :] = nn(c_out[...], wo[...]).astype(BF16)

        @pl.when(step == 1)
        def _():
            keep[...] = nn(c_out[0:BLK, :], wo[...]).astype(BF16)
            send[0:BLK, :] = nn(c_out[BLK:2 * BLK, :], wo[...]).astype(BF16)
    else:
        rest[5][...] = nn(c_out[...], wo[...]).astype(BF16)


def attend_fwd(first, steps, meta, lens, tokens, wq, wk, wv, bqv, wo):
    d, width = wq.shape
    n_pairs = width // 128
    seq = 2 * BLK
    rows = steps * seq

    def x_map(part):
        return lambda i, meta, lens: (meta[2 * (i + first) + part], 0)

    blk = pl.BlockSpec((seq, width), lambda i, *_: (i, 0))
    outs = [struct((rows, width), BF16)] * 4 + [struct((steps, 8, seq), F32)]
    specs = [blk] * 4 + [pl.BlockSpec((1, 8, seq), lambda i, *_: (i, 0, 0))]
    if first == 0:
        outs += [struct((3 * BLK, d), BF16), struct((BLK, d), BF16)]
        specs += [out_whole((3 * BLK, d)), out_whole((BLK, d))]
    else:
        outs += [struct((seq, d), BF16)]
        specs += [out_whole((seq, d))]
    return call(
        functools.partial(attend_fwd_kernel, n_pairs, first),
        f"attend_fwd_{first}",
        (steps,),
        2,
        [
            pl.BlockSpec((BLK, d), x_map(0)),
            pl.BlockSpec((BLK, d), x_map(1)),
            whole(wq.shape), whole(wk.shape), whole(wv.shape),
            whole((2, width)), whole(wo.shape),
        ],
        specs,
        outs,
        [pltpu.VMEM((d, 3 * width), BF16)],
        8 * rows * d * width + 8 * rows * seq * width,
        4 * rows * d + 8 * d * width + 10 * rows * width,
    )(meta, lens, tokens, tokens, wq, wk, wv, bqv, wo)


def phi_pair(u):
    size = jnp.abs(u)
    t = 1.0 / (1.0 + (0.3275911 * 0.7071067811865476) * size)
    e = jnp.exp(u * u * (-0.5))
    poly = t * (0.127414796 + t * (-0.142248368 + t * (0.7107068705 + t * (-0.7265760135 + t * 0.5307027145))))
    tail = poly * e
    phi = jnp.where(u >= 0, 1.0 - tail, tail)
    return u * phi, phi + u * (e * 0.3989422804014327)


def feed_forward_kernel(
    meta, tok, keep_a, keep_b, recv, cot, wup_o, wup_r, wdn_o, wdn_r, bups, wproj, vecs, bproj,
    active, pre_out, hlow, dlow, mix, emb_out, gproj, sums, psum, usum,
    wup, wdn, slope, h_one, xhat_one, rstd_one, acc, pre, rstd_two, gtwo, hfin, acc8, gp_acc, sems,
):
    step = pl.program_id(0)
    d = tok.shape[1]
    half = wup_o.shape[1]
    copies = (
        pltpu.make_async_copy(wup_o, wup.at[0], sems.at[0]),
        pltpu.make_async_copy(wup_r, wup.at[1], sems.at[1]),
        pltpu.make_async_copy(wdn_o, wdn.at[0], sems.at[2]),
        pltpu.make_async_copy(wdn_r, wdn.at[1], sems.at[3]),
    )

    @pl.when(step == 0)
    def _():
        for item in (0, 2, 1, 3):
            copies[item].start()
        acc8[...] = jnp.zeros_like(acc8)
        gp_acc[...] = jnp.zeros_like(gp_acc)
        psum[...] = jnp.zeros_like(psum)
        usum[...] = jnp.zeros_like(usum)

    chunk = 32
    first = step == 0

    @pl.loop(0, BLK // chunk, unroll=8)
    def _(it):
        rows = pl.ds(pl.multiple_of(it * chunk, chunk), chunk)
        mine = jnp.where(first, keep_a[rows, :].astype(F32), keep_b[rows, :].astype(F32))
        r = tok[rows, :].astype(F32) + (mine + recv[rows, :].astype(F32)) + vecs[0:1, :]
        center = r - jnp.mean(r, axis=-1, keepdims=True)
        rstd = lax.rsqrt(jnp.mean(center * center, axis=-1, keepdims=True) + EPS_NORM)
        xhat = center * rstd
        h = xhat * vecs[1:2, :] + vecs[2:3, :]
        h_one[rows, :] = h
        hlow[rows, :] = h.astype(BF16)
        xhat_one[rows, :] = xhat
        rstd_one[rows, :] = jnp.broadcast_to(rstd, (chunk, 128))

    tile = 512
    per = half // tile
    n_tiles = 2 * per

    def up(j, slot):
        who, col = j // per, (j % per) * tile
        if per and j % per == 0:
            @pl.when(first)
            def _():
                copies[who].wait()
        pre[slot] = nn(hlow[...], wup[who, :, col:col + tile])

    def act(j, slot):
        out = j * tile
        bias = bups[:, out:out + tile]
        for r in range(0, BLK, 16):
            value, grad = phi_pair(pre[slot, r:r + 16, :] + bias)
            active[r:r + 16, out:out + tile] = value.astype(BF16)
            slope[r:r + 16, out:out + tile] = grad.astype(BF16)

    def down(j):
        who, row = j // per, (j % per) * tile
        if j % per == 0:
            @pl.when(first)
            def _():
                copies[2 + who].wait()
        part = nn(active[:, j * tile:(j + 1) * tile], wdn[who, row:row + tile, :])
        if j == 0:
            acc[...] = part
        else:
            acc[...] += part

    up(0, 0)
    for j in range(n_tiles):
        if j + 1 < n_tiles:
            up(j + 1, (j + 1) % 2)
        act(j, j % 2)
        down(j)

    @pl.loop(0, BLK // chunk, unroll=8)
    def _(it):
        rows = pl.ds(pl.multiple_of(it * chunk, chunk), chunk)
        r = h_one[rows, :] + acc[rows, :] + vecs[3:4, :]
        center = r - jnp.mean(r, axis=-1, keepdims=True)
        rstd = lax.rsqrt(jnp.mean(center * center, axis=-1, keepdims=True) + EPS_NORM)
        xhat = center * rstd
        acc[rows, :] = xhat
        rstd_two[rows, :] = jnp.broadcast_to(rstd, (chunk, 128))
        hfin[rows, :] = (xhat * vecs[4:5, :] + vecs[5:6, :]).astype(BF16)

    emb = nn(hfin[...], wproj[...]) + bproj[...]
    norm = lax.rsqrt(jnp.sum(emb * emb, axis=-1, keepdims=True) + EPS_UNIT)
    unit = emb * norm
    emb_out[...] = unit.astype(BF16)
    c = cot[...].astype(F32)
    ge = norm * (c - unit * jnp.sum(unit * c, axis=-1, keepdims=True))
    psum[...] += jnp.sum(ge.reshape(BLK // 8, 8, 128), axis=0)
    gelow = ge.astype(BF16)
    gp_acc[...] += tn(gelow, hfin[...])
    gtwo[...] = nt(gelow, wproj[...])

    @pl.loop(0, BLK // chunk, unroll=8)
    def _(it):
        rows = pl.ds(pl.multiple_of(it * chunk, chunk), chunk)
        dy = gtwo[rows, :]
        xhat = acc[rows, :]
        dz = dy * vecs[4:5, :]
        m_one = jnp.mean(dz, axis=-1, keepdims=True)
        m_two = jnp.mean(dz * xhat, axis=-1, keepdims=True)
        gr = (dz - m_one - xhat * m_two) * rstd_two[rows, 0:1]
        gtwo[rows, :] = gr
        dlow[rows, :] = gr.astype(BF16)
        acc8[0] += jnp.sum(gr.reshape(chunk // 8, 8, d), axis=0)
        acc8[1] += jnp.sum((dy * xhat).reshape(chunk // 8, 8, d), axis=0)
        acc8[2] += jnp.sum(dy.reshape(chunk // 8, 8, d), axis=0)

    def up_back(j, slot):
        who, row = j // per, (j % per) * tile
        pre[slot] = nt(dlow[...], wdn[who, row:row + tile, :])

    def act_back(j, slot):
        cols = slice(j * tile, (j + 1) * tile)
        total = jnp.zeros((8, tile), F32)
        for r in range(0, BLK, 16):
            grad = pre[slot, r:r + 16, :] * slope[r:r + 16, cols].astype(F32)
            pre_out[r:r + 16, cols] = grad.astype(BF16)
            total = total + (grad[0:8] + grad[8:16])
        usum[:, cols] += total

    def down_back(j):
        who, col = j // per, (j % per) * tile
        part = nt(pre_out[:, j * tile:(j + 1) * tile], wup[who, :, col:col + tile])
        if j == 0:
            acc[...] = part
        else:
            acc[...] += part

    up_back(0, 0)
    for j in range(n_tiles):
        if j + 1 < n_tiles:
            up_back(j + 1, (j + 1) % 2)
        act_back(j, j % 2)
        down_back(j)

    @pl.loop(0, BLK // chunk, unroll=8)
    def _(it):
        rows = pl.ds(pl.multiple_of(it * chunk, chunk), chunk)
        dy = acc[rows, :] + gtwo[rows, :]
        xhat = xhat_one[rows, :]
        dz = dy * vecs[1:2, :]
        m_one = jnp.mean(dz, axis=-1, keepdims=True)
        m_two = jnp.mean(dz * xhat, axis=-1, keepdims=True)
        gr = (dz - m_one - xhat * m_two) * rstd_one[rows, 0:1]
        mix[rows, :] = gr.astype(BF16)
        acc8[3] += jnp.sum(gr.reshape(chunk // 8, 8, d), axis=0)
        acc8[4] += jnp.sum((dy * xhat).reshape(chunk // 8, 8, d), axis=0)
        acc8[5] += jnp.sum(dy.reshape(chunk // 8, 8, d), axis=0)

    @pl.when(step == pl.num_programs(0) - 1)
    def _():
        gproj[...] = gp_acc[...].astype(BF16)
        for row in range(6):
            sums[row:row + 1, :] = jnp.sum(acc8[row], axis=0, keepdims=True)
        sums[6:8, :] = jnp.zeros((2, d), F32)


def feed_forward(meta, tokens, keep_a, keep_b, recv, cot, wup_o, wup_r, wdn_o, wdn_r, bup_o, bup_r, wproj, vecs, bproj):
    d, half = wup_o.shape
    rows = 3 * BLK
    proj = wproj.shape[1]
    row_map = lambda i, meta: (i, 0)
    tok_map = lambda i, meta: (meta[jnp.where(i == 0, 2, 3 + i)], 0)
    any_spec = pl.BlockSpec(memory_space=ANY)
    return call(
        feed_forward_kernel,
        "feed_forward",
        (3,),
        1,
        [
            pl.BlockSpec((BLK, d), tok_map),
            whole((BLK, d)),
            pl.BlockSpec((BLK, d), lambda i, meta: (jnp.maximum(i - 1, 0), 0)),
            pl.BlockSpec((BLK, d), row_map),
            pl.BlockSpec((BLK, proj), tok_map),
            any_spec, any_spec, any_spec, any_spec,
            whole((1, 2 * half)),
            whole(wproj.shape), whole((8, d)), whole((1, proj)),
        ],
        [
            pl.BlockSpec((BLK, 2 * half), row_map),
            pl.BlockSpec((BLK, 2 * half), row_map),
            pl.BlockSpec((BLK, d), row_map),
            pl.BlockSpec((BLK, d), row_map),
            pl.BlockSpec((BLK, d), row_map),
            pl.BlockSpec((BLK, proj), row_map),
            out_whole((proj, d)),
            out_whole((8, d)),
            out_whole((8, proj)),
            out_whole((8, 2 * half)),
        ],
        [
            struct((rows, 2 * half), BF16),
            struct((rows, 2 * half), BF16),
            struct((rows, d), BF16),
            struct((rows, d), BF16),
            struct((rows, d), BF16),
            struct((rows, proj), BF16),
            struct((proj, d), BF16),
            struct((8, d), F32),
            struct((8, proj), F32),
            struct((8, 2 * half), F32),
        ],
        [
            pltpu.VMEM((2, d, half), BF16),
            pltpu.VMEM((2, half, d), BF16),
            pltpu.VMEM((BLK, 2 * half), BF16),
            pltpu.VMEM((BLK, d), F32),
            pltpu.VMEM((BLK, d), F32),
            pltpu.VMEM((BLK, 128), F32),
            pltpu.VMEM((BLK, d), F32),
            pltpu.VMEM((2, BLK, 512), F32),
            pltpu.VMEM((BLK, 128), F32),
            pltpu.VMEM((BLK, d), F32),
            pltpu.VMEM((BLK, d), BF16),
            pltpu.VMEM((6, 8, d), F32),
            pltpu.VMEM((proj, d), F32),
            pltpu.SemaphoreType.DMA((4,)),
        ],
        16 * rows * d * half + 6 * rows * d * proj,
        8 * d * half + 8 * rows * half + 12 * rows * d,
    )(
        meta, tokens, keep_a, keep_b, recv, cot, wup_o, wup_r, wdn_o, wdn_r,
        jnp.concatenate([bup_o, bup_r]).reshape(1, -1), wproj, vecs, bproj.reshape(1, -1),
    )


def down_other_kernel(act, dlow, out):
    out[...] = tn(act[...], dlow[...]).astype(BF16)


def down_other(active, dlow):
    rows, d = dlow.shape
    half = active.shape[1] // 2
    tile = 256
    shift = half // tile
    return call(
        down_other_kernel,
        "grad_down_other",
        (half // tile,),
        0,
        [pl.BlockSpec((rows, tile), lambda i: (0, shift + i)), whole((rows, d))],
        pl.BlockSpec((tile, d), lambda i: (i, 0)),
        struct((half, d), BF16),
        [],
        2 * rows * d * half,
        2 * rows * half + 2 * rows * d + 2 * half * d,
    )(active, dlow)


def spread(source, me, shards, rows, outs, at=0):
    middle = shards // 2
    for place in range(shards):
        start = pl.multiple_of(jnp.bitwise_xor(place, me) * rows, 8)
        target = outs[place // middle]
        target[place % middle, at:at + rows, :] = source[pl.ds(start, rows), :].astype(BF16)


def down_own_kernel(shards, ids, act, dlow, recv, gproj, grecv, keep_a, send_a, keep_b, send_b, full, extra):
    step = pl.program_id(0)
    tile = act.shape[1]
    rows = pl.ds(pl.multiple_of(step * tile, tile), tile)
    full[rows, :] = (tn(act[...], dlow[...]) + recv[...].astype(F32)).astype(BF16)

    @pl.when(step == pl.num_programs(0) - 1)
    def _():
        part = full.shape[0] // 2
        per = part // shards
        spread(full.at[0:part], ids[0], shards, per, (keep_a, send_a))
        extra[...] = gproj[...].astype(F32) + grecv[...].astype(F32)
        spread(extra, ids[0], shards, extra.shape[0] // shards, (keep_a, send_a), at=per)
        spread(full.at[part:2 * part], ids[1], shards, per, (keep_b, send_b))


def down_own(shards, ids, active, dlow, recv, gproj, grecv):
    rows, d = dlow.shape
    half = active.shape[1] // 2
    tile = 256
    per = half // 2 // shards
    extra = gproj.shape[0] // shards
    shape_a, shape_b = (shards // 2, per + extra, d), (shards // 2, per, d)
    return call(
        functools.partial(down_own_kernel, shards),
        "grad_down_own",
        (half // tile,),
        1,
        [
            pl.BlockSpec((rows, tile), lambda i, ids: (0, i)),
            whole((rows, d)),
            pl.BlockSpec((tile, d), lambda i, ids: (i, 0)),
            whole(gproj.shape),
            whole(gproj.shape),
        ],
        [out_whole(shape_a)] * 2 + [out_whole(shape_b)] * 2,
        [struct(shape_a, BF16)] * 2 + [struct(shape_b, BF16)] * 2,
        [pltpu.VMEM((half, d), BF16), pltpu.VMEM(gproj.shape, F32)],
        2 * rows * d * half,
        2 * rows * half + 2 * rows * d + 4 * half * d,
    )(ids, active, dlow, recv, gproj, grecv)


def up_other_kernel(hlow, pre, out, flipped):
    @pl.when(pl.program_id(0) == 0)
    def _():
        flipped[...] = jnp.transpose(hlow[...])

    out[...] = nn(flipped[...], pre[...]).astype(BF16)


def up_other(hlow, pre):
    rows, d = hlow.shape
    half = pre.shape[1] // 2
    tile = 512
    shift = half // tile
    return call(
        up_other_kernel,
        "grad_up_other",
        (half // tile,),
        0,
        [whole((rows, d)), pl.BlockSpec((rows, tile), lambda i: (0, shift + i))],
        pl.BlockSpec((d, tile), lambda i: (0, i)),
        struct((d, half), BF16),
        [pltpu.VMEM((d, rows), BF16)],
        2 * rows * d * half,
        2 * rows * half + 2 * rows * d + 2 * half * d,
    )(hlow, pre)


def up_own_kernel(shards, ids, hlow, pre, recv, keep_a, send_a, keep_b, send_b, flipped, full):
    step = pl.program_id(0)
    d = hlow.shape[1]
    tile = pre.shape[1]
    per = d // shards

    @pl.when(step == 0)
    def _():
        flipped[...] = jnp.transpose(hlow[...])

    out = (nn(flipped[...], pre[...]) + recv[...].astype(F32)).astype(BF16)
    full[...] = out
    steps = pl.num_programs(0) // 2
    for part, outs in ((0, (keep_a, send_a)), (1, (keep_b, send_b))):
        for place in range(2):
            @pl.when(step == part * 2 + place)
            def _(part=part, outs=outs, place=place):
                for j in range(shards):
                    start = pl.multiple_of(jnp.bitwise_xor(j, ids[part]) * per, 8)
                    outs[j // (shards // 2)][j % (shards // 2), :, place * tile:(place + 1) * tile] = full[
                        pl.ds(start, per), :
                    ]


def up_own(shards, ids, hlow, pre, recv):
    rows, d = hlow.shape
    half = pre.shape[1] // 2
    tile = half // 4
    shape = (shards // 2, d // shards, half // 2)
    return call(
        functools.partial(up_own_kernel, shards),
        "grad_up_own",
        (4,),
        1,
        [
            whole((rows, d)),
            pl.BlockSpec((rows, tile), lambda i, ids: (0, i)),
            pl.BlockSpec((d, tile), lambda i, ids: (0, i)),
        ],
        [out_whole(shape)] * 4,
        [struct(shape, BF16)] * 4,
        [pltpu.VMEM((d, rows), BF16), pltpu.VMEM((d, tile), BF16)],
        2 * rows * d * half,
        2 * rows * half + 2 * rows * d + 4 * half * d,
    )(ids, hlow, pre, recv)


def attend_bwd_kernel(n_pairs, passage, meta, lens, q, k, v, ctx, lse, mix0, mix1, wq, wk, wv, wo, *rest):
    dqkv, dx, sums, gctx, wcat, deltas, lser = rest
    width = n_pairs * 128
    seq = 2 * BLK
    wcat[:, 0:width] = wq[...]
    wcat[:, width:2 * width] = wk[...]
    wcat[:, 2 * width:3 * width] = wv[...]
    for part, mix in ((0, mix0), (1, mix1)):
        gctx[part * BLK:(part + 1) * BLK, :] = nt(mix[...], wo[...]).astype(BF16)
    length = lens[meta[6 + passage]]
    place = lax.broadcasted_iota(jnp.int32, (seq, 1), 0)
    if passage == 1:
        place = jnp.where(place < BLK, place + meta[9], place + meta[10] - BLK)
    bias = jnp.where(place < length, 0.0, MASKED)
    both = gctx[...].astype(F32) * ctx[...].astype(F32)
    high = both.astype(BF16)
    low = (both - high.astype(F32)).astype(BF16)
    owner = lax.broadcasted_iota(jnp.int32, (16, width), 1) // HEAD
    member = (owner == lax.broadcasted_iota(jnp.int32, (16, width), 0)).astype(F32).astype(BF16)
    deltas[...] = (nt(member, high) + nt(member, low))[0:8, :]
    lser[...] = lse[0]
    for pair in range(n_pairs):
        cols = slice(pair * 128, (pair + 1) * 128)
        qp, kp, vp, gp = q[:, cols], k[:, cols], v[:, cols], gctx[:, cols]
        kflip = jnp.transpose(kp)
        dk = dv = dq = None
        for head in range(2):
            lanes = pair_lanes(head)
            here = 2 * pair + head
            qm = jnp.where(lanes, qp, jnp.zeros_like(qp))
            gm = jnp.where(lanes, gp, jnp.zeros_like(gp))
            probs = jnp.exp(nt(kp, qm) + bias - lser[here:here + 1, :])
            dprobs = nt(vp, gm)
            dscores = (probs * (dprobs - deltas[here:here + 1, :])).astype(BF16)
            dv_part = nn(probs.astype(BF16), gm)
            dk_part = nn(dscores, qm)
            dq_part = nn(kflip, dscores)
            if head == 0:
                dk, dv, dq = dk_part, dv_part, dq_part
            else:
                row = lax.broadcasted_iota(jnp.int32, (128, 1), 0)
                dk, dv, dq = dk + dk_part, dv + dv_part, jnp.where(row < HEAD, dq, dq_part)
        dq = jnp.transpose(dq) * 0.125
        sums[0:1, cols] = jnp.sum(dq, axis=0, keepdims=True)
        sums[1:2, cols] = jnp.sum(dv, axis=0, keepdims=True)
        dqkv[:, cols] = dq.astype(BF16)
        dqkv[:, width + pair * 128:width + (pair + 1) * 128] = dk.astype(BF16)
        dqkv[:, 2 * width + pair * 128:2 * width + (pair + 1) * 128] = dv.astype(BF16)
    sums[2:8, :] = jnp.zeros((6, width), F32)
    for part in range(2):
        rows = slice(part * BLK, (part + 1) * BLK)
        dx[rows, :] = nt(dqkv[rows, :], wcat[...]).astype(BF16)


def attend_bwd(passage, meta, lens, saved, own, recv, wq, wk, wv, wo):
    d, width = wq.shape
    n_pairs = width // 128
    seq = 2 * BLK
    q, k, v, ctx, lse = saved
    at = passage if passage < 2 else 0
    blk = pl.BlockSpec((seq, width), lambda i, *_: (at, 0))
    first, second = [((recv, 1), (recv, 2)), ((own, 0), (recv, 0)), ((own, 1), (own, 2))][passage]

    def mix_spec(index):
        return pl.BlockSpec((BLK, d), lambda i, *_: (index, 0))

    return call(
        functools.partial(attend_bwd_kernel, n_pairs, passage),
        f"attend_bwd_{passage}",
        (1,),
        2,
        [
            blk, blk, blk, blk,
            pl.BlockSpec((1, 8, seq), lambda i, *_: (at, 0, 0)),
            mix_spec(first[1]), mix_spec(second[1]),
            whole(wq.shape), whole(wk.shape), whole(wv.shape), whole(wo.shape),
        ],
        [out_whole((seq, 3 * width)), out_whole((seq, d)), out_whole((8, width))],
        [struct((seq, 3 * width), BF16), struct((seq, d), BF16), struct((8, width), F32)],
        [
            pltpu.VMEM((seq, width), BF16),
            pltpu.VMEM((d, 3 * width), BF16),
            pltpu.VMEM((8, seq), F32),
            pltpu.VMEM((8, seq), F32),
        ],
        8 * seq * d * width + 20 * seq * seq * width,
        8 * d * width + 16 * seq * width + 4 * seq * d,
    )(meta, lens, q, k, v, ctx, lse, first[0], second[0], wq, wk, wv, wo)


def attn_weights_kernel(
    shards, meta, ids, x0, x1, g0, g1, g2, c0, c1, m0, m1, vec, keep_a, send_a, keep_b, send_b, acc, acc_o, full
):
    step = pl.program_id(0)
    width = c0.shape[1]
    d = x0.shape[1]

    def add(x, grads, ctx, mix, rows, first):
        part = tn(x[...], grads[rows, :])
        part_o = tn(ctx[rows, :], mix)
        if first:
            acc[...] = part
            acc_o[...] = part_o
        else:
            acc[...] += part
            acc_o[...] += part_o

    lo, hi = slice(0, BLK), slice(BLK, 2 * BLK)
    blk = lambda ref, i: ref[i * BLK:(i + 1) * BLK, :]
    own, recv = m0, m1

    @pl.when(step == 0)
    def _():
        add(x0, g0, c0, blk(recv, 1), lo, True)
        add(x1, g0, c0, blk(recv, 2), hi, False)

    @pl.when(step == 1)
    def _():
        mid_lo, mid_hi = slice(2 * BLK, 3 * BLK), slice(3 * BLK, 4 * BLK)
        acc[...] += tn(x0[...], g1[lo, :]) + tn(x1[...], g1[hi, :])
        acc_o[...] += tn(c0[mid_lo, :], blk(own, 0)) + tn(c0[mid_hi, :], blk(recv, 0))

    @pl.when(step == 2)
    def _():
        add(x0, g2, c1, blk(own, 1), lo, False)
        add(x1, g2, c1, blk(own, 2), hi, False)
        full[:, 0:2 * width] = acc[:, 0:2 * width].astype(BF16)
        spread(full, ids[0], shards, d // shards, (keep_a, send_a))
        spread(vec, ids[0], shards, vec.shape[0] // shards, (keep_a, send_a), at=d // shards)
        full[:, 0:width] = acc[:, 2 * width:3 * width].astype(BF16)
        full[0:width, width:2 * width] = acc_o[:, 0:width].astype(BF16)
        full[width:2 * width, width:2 * width] = acc_o[:, width:2 * width].astype(BF16)
        spread(full, ids[1], shards, d // shards, (keep_b, send_b))


def attn_weights(shards, meta, ids, tokens, grads, ctx_a, ctx_b, own, recv, vec):
    d = tokens.shape[1]
    width = ctx_a.shape[1]
    seq = 2 * BLK
    shape_b = (shards // 2, d // shards, 2 * width)
    shape_a = (shards // 2, d // shards + vec.shape[0] // shards, 2 * width)
    rows = 3 * seq

    def x_map(part):
        return lambda i, meta, ids: (meta[2 * i + part], 0)

    return call(
        functools.partial(attn_weights_kernel, shards),
        "attn_weights",
        (3,),
        2,
        [
            pl.BlockSpec((BLK, d), x_map(0)),
            pl.BlockSpec((BLK, d), x_map(1)),
            whole((seq, 3 * width)), whole((seq, 3 * width)), whole((seq, 3 * width)),
            whole(ctx_a.shape), whole(ctx_b.shape),
            whole(own.shape), whole(recv.shape), whole(vec.shape),
        ],
        [out_whole(shape_a)] * 2 + [out_whole(shape_b)] * 2,
        [struct(shape_a, BF16)] * 2 + [struct(shape_b, BF16)] * 2,
        [pltpu.VMEM((d, 3 * width), F32), pltpu.VMEM((width, d), F32), pltpu.VMEM((d, 2 * width), BF16)],
        8 * rows * d * width,
        4 * rows * d + 8 * rows * width + 8 * d * width,
    )(meta, ids, tokens, tokens, grads[0], grads[1], grads[2], ctx_a, ctx_b, own, recv, vec)


def after(value, *tokens):
    leaves, tree = jax.tree.flatten(value)
    out = lax.optimization_barrier((*leaves, *tokens))
    return jax.tree.unflatten(tree, out[: len(leaves)])


def exchange(value, bit, n_data):
    return lax.ppermute(value, "dp", [(i, i ^ bit) for i in range(n_data)])


def add_low(a, b):
    return (a.astype(F32) + b.astype(F32)).astype(BF16)


class Chain:
    def __init__(self, parts, orders, n_data):
        self.orders, self.n_data = orders, n_data
        self.hop = 0
        self.keep = [keep for keep, _ in parts]
        self.send([send for _, send in parts])

    def bit(self, part):
        order = self.orders[part]
        return (order + order[::-1])[self.hop]

    def send(self, values):
        self.token = values[-1]
        self.got = [exchange(value, self.bit(i), self.n_data) for i, value in enumerate(values)]
        self.hop += 1

    def advance(self, *tokens):
        self.keep, self.got = after((self.keep, self.got), *tokens)
        hops = len(self.orders[0])
        if self.hop < hops:
            half = [keep.shape[0] // 2 for keep in self.keep]
            sends = [add_low(k[h:], g[h:]) for k, g, h in zip(self.keep, self.got, half)]
            self.keep = [add_low(k[:h], g[:h]) for k, g, h in zip(self.keep, self.got, half)]
            self.send(sends)
        elif self.hop == hops:
            self.keep = [add_low(k, g) for k, g in zip(self.keep, self.got)]
            self.send(self.keep)
        elif self.hop < 2 * hops:
            self.keep = [jnp.concatenate([k, g]) for k, g in zip(self.keep, self.got)]
            self.send(self.keep)
        return self.token

    def result(self):
        return list(zip(self.keep, self.got))


class Plain:
    def __init__(self, parts):
        sums = [lax.psum(jnp.concatenate(part), "dp") for part in parts]
        self.pairs = [(total[: total.shape[0] // 2], total[total.shape[0] // 2:]) for total in sums]
        self.token = sums[-1]

    def advance(self, *tokens):
        return self.token

    def result(self):
        return self.pairs


def place_id(bits):
    me = lax.axis_index("dp")
    value = 0
    for bit in bits:
        value = value * 2 + jnp.where(jnp.bitwise_and(me, bit) != 0, 1, 0)
    return value


def picked(low, high, place, half, rows):
    at = jnp.bitwise_and(place, half - 1)
    return jnp.where(place < half, low[at, rows, :].astype(F32), high[at, rows, :].astype(F32))


def unpack_down_kernel(shards, per, ids, low_a, high_a, low_b, high_b, out, extra):
    step = pl.program_id(0)
    half, group = shards // 2, shards // 4
    more = low_a.shape[1] - per
    for part, (low, high) in enumerate(((low_a, high_a), (low_b, high_b))):
        @pl.when(step // 4 == part)
        def _(part=part, low=low, high=high):
            for q in range(group):
                shard = (step % 4) * group + q
                place = jnp.bitwise_xor(shard, ids[part])
                out[q * per:(q + 1) * per, :] = picked(low, high, place, half, slice(0, per))
                if part == 0:
                    rows = pl.ds(pl.multiple_of(shard * more, more), more)
                    extra[rows, :] = picked(low, high, place, half, slice(per, per + more))


def unpack_down(shards, ids, parts):
    args = [array for part in parts for array in part]
    d = args[0].shape[2]
    per = args[2].shape[1]
    more = args[0].shape[1] - per
    rows = 2 * shards * per
    return call(
        functools.partial(unpack_down_kernel, shards, per),
        "unpack_down",
        (8,),
        1,
        [whole(array.shape) for array in args],
        [pl.BlockSpec((rows // 8, d), lambda i, ids: (i, 0)), out_whole((shards * more, d))],
        [struct((rows, d), F32), struct((shards * more, d), F32)],
        [],
        rows * d,
        6 * rows * d,
    )(ids, *args)


def unpack_up_kernel(shards, ids, low_a, high_a, low_b, high_b, out):
    step = pl.program_id(0)
    half, group = shards // 2, shards // 4
    per, wide = low_a.shape[1:]
    for part, (low, high) in enumerate(((low_a, high_a), (low_b, high_b))):
        for q in range(group):
            place = jnp.bitwise_xor(step * group + q, ids[part])
            out[q * per:(q + 1) * per, part * wide:(part + 1) * wide] = picked(low, high, place, half, slice(None))


def unpack_up(shards, ids, parts):
    args = [array for part in parts for array in part]
    per, wide = args[0].shape[1:]
    rows = shards * per
    return call(
        functools.partial(unpack_up_kernel, shards),
        "unpack_up",
        (4,),
        1,
        [whole(array.shape) for array in args],
        pl.BlockSpec((rows // 4, 2 * wide), lambda i, ids: (i, 0)),
        struct((rows, 2 * wide), F32),
        [],
        2 * rows * wide,
        12 * rows * wide,
    )(ids, *args)


def unpack_attn_kernel(shards, per, ids, low_a, high_a, low_b, high_b, query, key, value, out, vec):
    step = pl.program_id(0)
    half, group = shards // 2, shards // 4
    width = low_b.shape[2] // 2
    more = low_a.shape[1] - per
    every = slice(None)
    for q in range(group):
        shard = step * group + q
        rows = slice(q * per, (q + 1) * per)
        place = jnp.bitwise_xor(shard, ids[0])
        both = picked(low_a, high_a, place, half, slice(0, per))
        query[rows, :], key[rows, :] = both[:, :width], both[:, width:]
        vec[q * more:(q + 1) * more, :] = picked(low_a, high_a, place, half, slice(per, per + more))
        value[rows, :] = picked(low_b, high_b, jnp.bitwise_xor(shard, ids[1]), half, every)[:, :width]
    for q in range(group // 2):
        rows = slice(q * per, (q + 1) * per)
        for side in range(2):
            shard = step * (group // 2) + q + side * half
            both = picked(low_b, high_b, jnp.bitwise_xor(shard, ids[1]), half, every)
            out[rows, side * width:(side + 1) * width] = both[:, width:]


def unpack_attn(shards, ids, parts):
    args = [array for part in parts for array in part]
    per, wide = args[2].shape[1:]
    more = args[0].shape[1] - per
    rows, width = shards * per, wide // 2
    spec = pl.BlockSpec((rows // 4, width), lambda i, ids: (i, 0))
    return call(
        functools.partial(unpack_attn_kernel, shards, per),
        "unpack_attn",
        (4,),
        1,
        [whole(array.shape) for array in args],
        [
            spec, spec, spec,
            pl.BlockSpec((width // 4, rows), lambda i, ids: (i, 0)),
            pl.BlockSpec((shards * more // 4, wide), lambda i, ids: (i, 0)),
        ],
        [struct((rows, width), F32)] * 3 + [struct((width, rows), F32), struct((shards * more, wide), F32)],
        [],
        2 * rows * wide,
        12 * rows * wide,
    )(ids, *args)


def finish_kernel(meta, own, other, out):
    step = pl.program_id(0)
    rows = pl.ds(pl.multiple_of(meta[17 + step] * BLK, BLK), BLK)
    out[...] = jnp.where(meta[11 + step] == 1, own[rows, :].astype(F32), other[rows, :].astype(F32))


def finish_tokens(meta, own, other):
    rows, d = own.shape
    return call(
        finish_kernel,
        "grad_tokens",
        (2 * rows // BLK,),
        1,
        [whole((rows, d)), whole((rows, d))],
        pl.BlockSpec((BLK, d), lambda i, meta: (i, 0)),
        struct((2 * rows, d), F32),
        [],
        rows * d,
        12 * rows * d,
    )(meta, own, other)


def body(
    tokens, lengths, w_query, b_query, w_key, w_value, b_value, w_out, b_out, gain_one, bias_one,
    w_up, b_up, w_down, b_down, gain_two, bias_two, w_proj, b_proj, cotangent,
):
    n_data = lax.axis_size("dp")
    core = lax.axis_index("tensor")
    d = tokens.shape[1]
    half = w_up.shape[1]
    swap = lambda value: lax.ppermute(value, "tensor", [(0, 1), (1, 0)])
    meta = jnp.array(
        [
            [4, 5, 2, 3, 0, 1, 2, 1, 0, 0, BLK, 1, 1, 1, 0, 0, 0, 1, 2, 0, 0, 1, 2],
            [0, 1, 3, 2, 4, 5, 0, 1, 2, BLK, 0, 0, 0, 0, 1, 1, 1, 1, 2, 0, 0, 1, 2],
        ],
        jnp.int32,
    )[core]

    wup_r, wdn_r, bup_r = swap(w_up), swap(w_down), swap(b_up)
    args = (meta, lengths, tokens, w_query, w_key, w_value, jnp.stack([b_query, b_value]), w_out)
    *saved_a, part_send, keep_a = attend_fwd(0, 2, *args)
    part_recv = swap(part_send)
    *saved_b, keep_b = attend_fwd(2, 1, *args)
    vecs = jnp.stack([b_out, gain_one, bias_one, b_down, gain_two, bias_two, b_out, b_out])
    active, pre, hlow, dlow, mix, emb, gproj, sums, sums_proj, sums_up = feed_forward(
        meta, tokens, keep_a, keep_b, part_recv, cotangent, w_up, wup_r, w_down, wdn_r, b_up, bup_r, w_proj, vecs, b_proj
    )
    mix_r = swap(mix)
    emb_r = swap(emb)

    if n_data == 16:
        bits_a, bits_b = (1, 4, 2, 8), (2, 4, 1, 8)
    else:
        bits_a = tuple(1 << b for b in range(n_data.bit_length() - 1))
        bits_b = bits_a
    shards = 16
    ids = jnp.stack([place_id(bits_a), place_id(bits_b)]).astype(jnp.int32)
    if n_data != shards:
        ids = jnp.zeros((2,), jnp.int32)

    def chain(keep_a, send_a, keep_b, send_b):
        parts = [(keep_a, send_a), (keep_b, send_b)]
        return Chain(parts, (bits_a, bits_b), n_data) if n_data == shards else Plain(parts)

    gproj_r = swap(gproj)
    down = down_other(active, dlow)
    down_r = swap(down)
    up = up_other(*after((hlow, pre), down))
    up_r = swap(up)
    ch_d = chain(*down_own(shards, ids, *after((active, dlow, down_r, gproj, gproj_r), up)))
    ch_u = chain(*up_own(shards, ids, *after((hlow, pre, up_r), ch_d.token)))
    token = ch_u.token

    up_sums = jnp.sum(sums_up, axis=0)
    shared = jnp.concatenate([sums[0:6].reshape(-1), jnp.sum(sums_proj, axis=0)])
    mine = jnp.concatenate([shared, up_sums[:half]])
    theirs_r = swap(jnp.concatenate([shared, up_sums[half:]]))

    weights = (w_query, w_key, w_value, w_out)
    bwd = []
    for s in range(3):
        *ins, emb_r = after((saved_a if s < 2 else saved_b, mix, mix_r, emb_r), token)
        bwd.append(attend_bwd(s, meta, lengths, *ins, *weights))
        token = bwd[-1][2]
        token = (ch_u if s == 1 else ch_d).advance(token)
    qv = bwd[0][2] + bwd[1][2] + bwd[2][2]
    flat = jnp.concatenate([mine + theirs_r, qv[0:2].reshape(-1)])
    size = flat.shape[0]
    room = -size % shards
    vec = jnp.pad(flat, (0, room)).reshape(shards, 1, -1)
    vec = jnp.pad(vec, ((0, 0), (0, 7), (0, d - vec.shape[2]))).reshape(8 * shards, d)
    away = jnp.concatenate([bwd[1][1][BLK:], bwd[0][1]], axis=0)
    home = jnp.concatenate([bwd[1][1][:BLK], bwd[2][1]], axis=0)
    away_r = swap(away)
    ins = after((tokens, [b[0] for b in bwd], saved_a[3], saved_b[3], mix, mix_r, vec), token)
    ch_a = chain(*attn_weights(shards, meta, ids, *ins))
    token = ch_u.advance(ch_d.advance(ch_a.token))

    for name in TAIL:
        if name in "dua":
            token = {"d": ch_d, "u": ch_u, "a": ch_a}[name].advance(token)
        elif name == "rows":
            home, away_r = after((home, away_r), token)
            grad_rows = (mix.astype(F32) + home.astype(F32) + away_r.astype(F32)).astype(BF16)
            grad_rows_r = swap(grad_rows)
            token = grad_rows
        elif name == "tokens":
            grad_tokens = finish_tokens(meta, *after((grad_rows, grad_rows_r), token))
            token = grad_tokens
        elif name == "emb":
            emb, emb_r = after((emb, emb_r), token)
            emb_pick = lambda a, b: jnp.where(core == 0, a, b)
            first = emb_pick(jnp.concatenate([emb[BLK:], emb[:BLK]]), jnp.concatenate([emb_r[BLK:], emb_r[:BLK]]))
            embeddings = jnp.concatenate([first, emb_pick(emb_r, emb)])
            token = embeddings
        elif name == "down":
            g_down, g_proj = unpack_down(shards, ids, after(ch_d.result(), token))
            token = g_proj
        elif name == "up":
            token = g_up = unpack_up(shards, ids, after(ch_u.result(), token))
    g_query, g_key, g_value, g_out, vec = unpack_attn(shards, ids, ch_a.result())
    flat = vec.reshape(shards, 8, d)[:, 0, : (size + room) // shards].reshape(-1)

    width = w_query.shape[1]
    part = lambda i: flat[i * d:(i + 1) * d]
    at = 6 * d + w_proj.shape[1]
    g_bup = flat[at:at + half]
    g_bq, g_bv = flat[at + half:at + half + width], flat[at + half + width:at + half + 2 * width]
    return (
        embeddings, grad_tokens, g_query, g_bq, g_key, g_value, g_bv, g_out,
        part(3), part(4), part(5), g_up, g_bup, g_down, part(0), part(1), part(2), g_proj.T, flat[6 * d:at],
    )


def solution(mesh):
    rows, cols, split = P("dp", None), P(None, "tensor"), P("tensor")
    return jax.shard_map(
        body,
        mesh=mesh,
        in_specs=(
            rows, P("dp"), cols, split, cols, cols, split, P("tensor", None), P(), P(), P(),
            cols, split, P("tensor", None), P(), P(), P(), P(), P(), rows,
        ),
        out_specs=(
            rows, rows, cols, split, cols, cols, split, P("tensor", None), P(), P(), P(),
            cols, split, P("tensor", None), P(), P(), P(), P(), P(),
        ),
        check_vma=False,
    )
```
